32 devices in a mesh: cam: 4 (over x, core), pt: 8 (over z, y).
Axes of the slice: x: 2, y: 2, z: 4, core: 2. Of those that a mesh axis runs over, the one named last changes fastest.
Arguments:
- right_side: float32 [9, 65536], P(None, ('cam', 'pt')), may hold values from -6 to 6
- cam_damping: float32 [9, 65536], P(None, ('cam', 'pt')), may hold values from 0.5 to 4
- point_damping: float32 [524288], P('pt'), may hold values from 0.1 to 1
- block_ids: int32 [4, 8, 64], P('cam', 'pt'), may hold values from 0 to 255, as said below
- slab_ids: int32 [4, 8, 64], P('cam', 'pt'), may hold values from 0 to 15
- cam_index: int32 [4, 8, 64, 4096], P('cam', 'pt'), may hold values from 0 to 63
- cam_jacobian: bfloat16 [4, 8, 64, 18, 4096], P('cam', 'pt'), may hold values from -0.59765625 to 0.59765625
- point_jacobian: bfloat16 [4, 8, 64, 6, 4096], P('cam', 'pt'), may hold values from -1.796875 to 1.796875
- pair_count: int32 [4, 8], P('cam', 'pt'), may hold values from 16 to 64, as said below
Outputs:
- solution: float32 [9, 65536], P(None, ('cam', 'pt'))
- residual: float32 [9, 65536], P(None, ('cam', 'pt'))
The draws below stay inside these ranges and needn't reach their ends.
Inputs may be any that keep to these rules, and one draw needn't show every extreme that they name: pair_count is 64 divided by a whole number from 1 to 4, rounded down; at least one device has all 64 slots used in every draw. The owner of a block is block_ids // 32; in every device's list at most 16 slots name blocks of one owner, and in every list some owner is named by exactly 16 slots.
All inputs are finite; a program needn't handle non-finite values.
Results may differ from the reference program's by a relative error of at most 0.0003.
Values sent between devices are 32-bit elements; how exact they have to be, the bound alone decides.
A program may use at most 128 MiB of HBM per device.

```python
import math
import jax
import jax.numpy as jnp
from jax import lax

BLOCK = 64
SLAB = 4096
ITERS = 2
BLK_DEV = 32
SLABS_PT = 16
PAIRS_DEV = 64
BLK_GRP = 256
CAP = 16
CAMERAS = 65536
POINTS = 524288
N_CAM = 4
N_PT = 8


def draw_pair_count(key, part):
    first_key, second_key = jax.random.split(key)
    divisor = jax.random.randint(first_key, (N_CAM * N_PT,), 1, 5)
    counts = PAIRS_DEV // divisor
    chosen = jax.random.randint(second_key, (), 0, N_CAM * N_PT)
    filled = jnp.where(jnp.arange(N_CAM * N_PT) == chosen, PAIRS_DEV, counts)
    return filled.reshape(N_CAM, N_PT).astype(jnp.int32)


def one_list(list_key):
    key_full, key_pick, key_order, key_local = jax.random.split(list_key, 4)
    busiest = jax.random.randint(key_full, (), 0, N_PT)
    others = (jnp.arange(N_PT - 1, dtype=jnp.int32) + busiest + 1) % N_PT
    pool = jax.random.permutation(key_pick, jnp.repeat(others, CAP))
    owners = jnp.concatenate([jnp.full((CAP,), busiest, jnp.int32), pool[:PAIRS_DEV - CAP]])
    owners = jax.random.permutation(key_order, owners)
    local = jax.random.randint(key_local, (PAIRS_DEV,), 0, BLK_DEV)
    return (owners * BLK_DEV + local).astype(jnp.int32)


def draw_block_ids(key, part):
    list_keys = jax.random.split(jax.random.fold_in(key, 17), N_CAM * N_PT)
    lists = jax.vmap(one_list)(list_keys)
    return lists.reshape(N_CAM, N_PT, PAIRS_DEV).astype(jnp.int32)


def plant(drawn, own_key, smallest, high):
    dims = drawn.shape
    index_at = [jax.random.randint(jax.random.fold_in(own_key, axis), (), 0, dims[axis]) for axis in range(len(dims))]
    drawn = drawn.at[tuple(index_at)].set(smallest)
    longest = dims.index(max(dims))
    index_at[longest] = (index_at[longest] + 1) % dims[longest]
    return drawn.at[tuple(index_at)].set(high)


def block_scale(rng, extent, cuts, smallest, largest):
    def one(position, shards_of):
        draws = jax.random.uniform(jax.random.fold_in(jax.random.fold_in(rng, 6), position), (shards_of,), jnp.float32, smallest / len(cuts), largest / len(cuts))
        return jnp.repeat(jnp.exp(draws), extent[position] // shards_of).reshape((-1,) + (1,) * (len(extent) - position - 1))

    loudness = one(*cuts[0])
    for cut in cuts[1:]:
        loudness = loudness * one(*cut)
    return loudness


def scatter_about(own_key, shape, spread, limit, cuts=(), held_as=jnp.bfloat16):
    result = spread * jax.random.normal(own_key, shape, jnp.float32)
    if cuts:
        result = result * block_scale(own_key, shape, cuts, -0.22, 0.18)
    return jnp.clip(result, -limit, limit).astype(held_as)


def setup_inputs(seed: int = 0) -> dict:
    streams_of = jax.random.split(jax.random.key(seed), 10)
    right_side = scatter_about(streams_of[0], (9, CAMERAS), 1.0, 6.0, ((1, 32),), jnp.float32)
    cam_damping = jnp.clip(jnp.exp(math.log(4.0) - 2.0794415 * jax.random.uniform(streams_of[1], (9, CAMERAS), jnp.float32) ** block_scale(streams_of[1], (9, CAMERAS), ((1, 32),), -0.2, 0.2)), 0.5, 4.0)
    point_damping = jnp.clip(jnp.exp(math.log(1.0) - 2.3025851 * jax.random.uniform(streams_of[2], (POINTS,), jnp.float32) ** block_scale(streams_of[2], (POINTS,), ((0, 8),), -0.2, 0.2)), 0.1, 1.0)
    block_ids = draw_block_ids(jax.random.fold_in(streams_of[9], 71), 0)
    slab_ids = plant(jax.random.randint(streams_of[4], (N_CAM, N_PT, PAIRS_DEV), 0, SLABS_PT), jax.random.fold_in(streams_of[4], 1), 0, SLABS_PT - 1).astype(jnp.int32)
    cam_index = plant(jax.random.randint(streams_of[5], (N_CAM, N_PT, PAIRS_DEV, SLAB), 0, BLOCK), jax.random.fold_in(streams_of[5], 1), 0, BLOCK - 1).astype(jnp.int32)
    cam_jacobian = scatter_about(streams_of[6], (N_CAM, N_PT, PAIRS_DEV, 18, SLAB), 0.1, 0.59765625, ((0, 4), (1, 8)))
    point_jacobian = scatter_about(streams_of[7], (N_CAM, N_PT, PAIRS_DEV, 6, SLAB), 0.3, 1.796875, ((0, 4), (1, 8)))
    pair_count = draw_pair_count(jax.random.fold_in(streams_of[9], 71), 0)
    return {"right_side": right_side, "cam_damping": cam_damping, "point_damping": point_damping, "block_ids": block_ids, "slab_ids": slab_ids, "cam_index": cam_index, "cam_jacobian": cam_jacobian, "point_jacobian": point_jacobian, "pair_count": pair_count}


HIGH = lax.Precision.HIGHEST


def hessian_terms(pt_jac):
    combos = [(0, 0), (0, 1), (0, 2), (1, 1), (1, 2), (2, 2)]
    return jnp.stack([jnp.sum(pt_jac[:, :, first].astype(jnp.float32) * pt_jac[:, :, second], axis=1) for first, second in combos], axis=1)


def collect(selector, terms):
    summed = jnp.einsum('ps,pkn->ksn', selector, terms, precision=HIGH)
    return summed.reshape(terms.shape[1], -1)


def invert_points(hess, damping):
    entry_xx = hess[0] + damping
    entry_xy = hess[1]
    entry_xz = hess[2]
    entry_yy = hess[3] + damping
    entry_yz = hess[4]
    entry_zz = hess[5] + damping
    cof_xx = entry_yy * entry_zz - entry_yz * entry_yz
    cof_xy = entry_xz * entry_yz - entry_xy * entry_zz
    cof_xz = entry_xy * entry_yz - entry_xz * entry_yy
    cof_yy = entry_xx * entry_zz - entry_xz * entry_xz
    cof_yz = entry_xy * entry_xz - entry_xx * entry_yz
    cof_zz = entry_xx * entry_yy - entry_xy * entry_xy
    determinant = entry_xx * cof_xx + entry_xy * cof_xy + entry_xz * cof_xz
    return jnp.stack([cof_xx, cof_xy, cof_xz, cof_yy, cof_yz, cof_zz]) / determinant


def apply_inverse(inverse, vector):
    out_x = inverse[0] * vector[0] + inverse[1] * vector[1] + inverse[2] * vector[2]
    out_y = inverse[1] * vector[0] + inverse[3] * vector[1] + inverse[4] * vector[2]
    out_z = inverse[2] * vector[0] + inverse[4] * vector[1] + inverse[5] * vector[2]
    return jnp.stack([out_x, out_y, out_z])


def project(cam_panel, blocks_here, index_here, cam_jac):
    grouped = cam_panel.reshape(9, -1, BLOCK).transpose(1, 0, 2)
    picked = grouped[blocks_here]
    at_camera = jnp.take_along_axis(picked, index_here[:, None, :], axis=2)
    return jnp.sum(cam_jac * at_camera[:, None], axis=2)


def reference(right_side, cam_damping, point_damping, block_ids, slab_ids, cam_index, cam_jacobian, point_jacobian, pair_count):
    devices_all = N_CAM * N_PT
    cam_grp = BLK_GRP * BLOCK
    npt = SLABS_PT * SLAB
    blocks_all = block_ids.reshape(devices_all, PAIRS_DEV)
    slabs_all = slab_ids.reshape(devices_all, PAIRS_DEV)
    index_all = cam_index.reshape(devices_all, PAIRS_DEV, SLAB)
    camjac_all = cam_jacobian.reshape(devices_all, PAIRS_DEV, 2, 9, SLAB)
    ptjac_all = point_jacobian.reshape(devices_all, PAIRS_DEV, 2, 3, SLAB)
    live_all = (jnp.arange(PAIRS_DEV, dtype=jnp.int32)[None, :] < pair_count.reshape(devices_all, 1)).astype(jnp.float32)
    slab_range = jnp.arange(SLABS_PT, dtype=jnp.int32)

    def selector_of(device):
        return (slabs_all[device][:, None] == slab_range[None, :]).astype(jnp.float32) * live_all[device][:, None]

    def hess_one(device):
        return collect(selector_of(device), hessian_terms(ptjac_all[device]))

    hess = lax.map(hess_one, jnp.arange(devices_all, dtype=jnp.int32))
    hess = jnp.sum(hess.reshape(N_CAM, N_PT, 6, npt), axis=0)
    inverse = jax.vmap(invert_points)(hess, point_damping.reshape(N_PT, npt))

    def schur(vector):
        groups = vector.reshape(9, N_CAM, cam_grp)

        def panel_of(device):
            return jnp.take(groups, device // N_PT, axis=1)

        def forward(device):
            projected = project(panel_of(device), blocks_all[device], index_all[device], camjac_all[device])
            pulled = jnp.sum(ptjac_all[device] * projected[:, :, None], axis=1)
            return collect(selector_of(device), pulled)

        point_parts = lax.map(forward, jnp.arange(devices_all, dtype=jnp.int32))
        point_sum = jnp.sum(point_parts.reshape(N_CAM, N_PT, 3, npt), axis=0)
        eliminated = jax.vmap(apply_inverse)(inverse, point_sum)

        def backward(device):
            cam_jac = camjac_all[device]
            pt_jac = ptjac_all[device]
            projected = project(panel_of(device), blocks_all[device], index_all[device], cam_jac)
            zpoint = jnp.take(eliminated, device % N_PT, axis=0).reshape(3, SLABS_PT, SLAB)
            pulled_back = jnp.moveaxis(zpoint[:, slabs_all[device], :], 0, 1)
            miss = projected - jnp.sum(pt_jac * pulled_back[:, None], axis=2)
            pushed = jnp.sum(cam_jac * miss[:, :, None], axis=1)
            flat_index = (jnp.arange(PAIRS_DEV, dtype=jnp.int32)[:, None] * BLOCK + index_all[device]).reshape(-1)
            values = pushed.transpose(0, 2, 1).reshape(-1, 9)
            cam_parts = jnp.zeros((PAIRS_DEV * BLOCK, 9), jnp.float32).at[flat_index].add(values)
            cam_parts = cam_parts.reshape(PAIRS_DEV, BLOCK, 9).transpose(0, 2, 1) * live_all[device][:, None, None]
            group_sum = jnp.zeros((BLK_GRP, 9, BLOCK), jnp.float32).at[blocks_all[device]].add(cam_parts)
            return group_sum.transpose(1, 0, 2).reshape(9, cam_grp)

        cam_all = lax.map(backward, jnp.arange(devices_all, dtype=jnp.int32))
        cam_all = jnp.sum(cam_all.reshape(N_CAM, N_PT, 9, cam_grp), axis=1)
        return cam_damping * vector + cam_all.transpose(1, 0, 2).reshape(9, CAMERAS)

    solution = jnp.zeros_like(right_side)
    residual = right_side
    direction = right_side
    norm_now = jnp.sum(residual * residual)
    for iteration in range(ITERS):
        image = schur(direction)
        step_size = norm_now / jnp.sum(direction * image)
        solution = solution + step_size * direction
        residual = residual - step_size * image
        norm_next = jnp.sum(residual * residual)
        direction = residual + (norm_next / norm_now) * direction
        norm_now = norm_next
    return solution, residual
```

```python
import functools

import jax
import jax.numpy as jnp
from jax import lax
from jax.experimental import pallas as pl
from jax.experimental.pallas import tpu as pltpu
from jax.sharding import PartitionSpec as P

BLOCK = 64
ITERS = 2
LANES = 128
CHUNKS = 4
COLS = 5 * LANES
F32 = jnp.float32
BF16 = jnp.bfloat16
VMEM_BYTES = 60 * 1024 * 1024
MESH = pl.DeviceIdType.MESH
HESS = [(0, 0), (1, 1), (2, 2), (0, 1), (1, 2), (0, 2)]


def iota(shape, axis):
    return lax.broadcasted_iota(jnp.int32, shape, axis)


def split2(value):
    high = value.astype(BF16)
    return high, (value - high.astype(F32)).astype(BF16)


def split3(value):
    high, low = split2(value)
    last = value - high.astype(F32) - low.astype(F32)
    return high, low, last.astype(BF16)


def dot(a, b):
    return jnp.dot(a, b, preferred_element_type=F32)


def select_rows(hot, value):
    parts = split3(value)
    return dot(hot, parts[0]) + dot(hot, parts[1]) + dot(hot, parts[2])


def invert(hess, damping):
    xx, yy, zz = (hess[k] + damping for k in range(3))
    xy, yz, xz = hess[3], hess[4], hess[5]
    cof_xx = yy * zz - yz * yz
    cof_xy = xz * yz - xy * zz
    cof_xz = xy * yz - xz * yy
    cof_yy = xx * zz - xz * xz
    cof_yz = xy * xz - xx * yz
    cof_zz = xx * yy - xy * xy
    det = xx * cof_xx + xy * cof_xy + xz * cof_xz
    return [c / det for c in (cof_xx, cof_xy, cof_xz, cof_yy, cof_yz, cof_zz)]


def apply_inverse(inv, vec):
    return [
        inv[0] * vec[0] + inv[1] * vec[1] + inv[2] * vec[2],
        inv[1] * vec[0] + inv[3] * vec[1] + inv[4] * vec[2],
        inv[2] * vec[0] + inv[4] * vec[1] + inv[5] * vec[2],
    ]


def body(
    ids_ref, slab_ref, count_ref, rs_ref, damp_ref, pdamp_ref, idx_hbm, jc_hbm, jp_hbm,
    answer_ref, residual_ref,
    idx, jc, jp, load_sem,
    place, place_t, pick, pick_t, sums_by_slab, slab_hot_t, asks_mine, asks,
    flat, v0, v1, v2, damp, packed, got, tables, proj, tbuf, zslot, pbuf, acc, slotsum,
    h_part, h_sib, h_red, h_far, inverse, y_part, y_sib, y_red, y_far, z_all,
    out_pack, in_pack, dots, dots_pt, dots_cam,
    ask_send, ask_recv, a_send, a_recv, e_send, e_recv,
    hs_sem, hx_sem, ys_sem, yx_sem, zx_sem, zs_sem, dp_sem, dc_sem,
):
    pairs, points = idx.shape
    owners = lax.axis_size("pt")
    ncam = lax.axis_size("cam")
    nx = ncam // 2
    me_pt = lax.axis_index("pt")
    me_cam = lax.axis_index("cam")
    me_x = me_cam // 2
    me_core = lax.rem(me_cam, 2)
    sibling = me_x * 2 + (1 - me_core)
    spots = 2 * pairs
    cap = spots // owners
    slabs = sums_by_slab.shape[0]
    width = points // CHUNKS
    part = width // ncam
    half = v0.shape[0] // 2
    row_tiles = points // LANES

    def far(hop):
        return lax.rem(me_x + hop, nx)

    def at_cam(cam):
        return {"cam": cam}

    def at_pt(pt):
        return {"pt": pt}

    loads = [
        pltpu.make_async_copy(jp_hbm, jp, load_sem.at[0]),
        pltpu.make_async_copy(idx_hbm, idx, load_sem.at[1]),
        pltpu.make_async_copy(jc_hbm, jc, load_sem.at[2]),
    ]
    for copy in loads:
        copy.start()

    barrier = pltpu.get_barrier_semaphore()
    for hop in range(1, owners):
        pl.semaphore_signal(
            barrier, inc=1, device_id=at_pt(lax.rem(me_pt + hop, owners)), device_id_type=MESH
        )
    for hop in range(1, ncam):
        pl.semaphore_signal(
            barrier, inc=1, device_id=at_cam(lax.rem(me_cam + hop, ncam)), device_id_type=MESH
        )

    square = (LANES, LANES)
    sub, lane = iota(square, 0), iota(square, 1)
    blank = jnp.zeros((1, LANES - pairs), F32)
    ids_row = jnp.concatenate([ids_ref[...].astype(F32), blank], axis=1)
    slab_row = jnp.concatenate([slab_ref[...].astype(F32), blank], axis=1)
    count = jnp.broadcast_to(count_ref[...], square)
    live_row = lane < count
    live_col = sub < count
    ids_row = jnp.broadcast_to(ids_row, square).astype(jnp.int32)
    slab_row = jnp.broadcast_to(slab_row, square)
    ids_col = ids_row.astype(F32).T.astype(jnp.int32)
    blocks_dev = 2 * half
    owner_row = ids_row // blocks_dev
    owner_col = ids_col // blocks_dev
    same = jnp.where(owner_row == owner_col, 1.0, 0.0)
    before = jnp.where((lane < sub) & live_row, same, 0.0)
    rank_col = jnp.broadcast_to(jnp.sum(before, axis=1, keepdims=True), square)
    pos_col = owner_col * cap + rank_col.astype(jnp.int32)
    pos_row = pos_col.astype(F32).T.astype(jnp.int32)
    pick_f = jnp.where((pos_row == sub) & live_row, 1.0, 0.0)
    pick_tf = jnp.where((pos_col == lane) & live_col, 1.0, 0.0)
    local = ids_row - owner_row * blocks_dev
    local = local // 2 + half * (local - (local // 2) * 2)
    asked = jnp.sum(pick_f * (local + 1).astype(F32), axis=1, keepdims=True) - 1.0
    asks_mine[...] = jnp.broadcast_to(asked, square).reshape(owners, cap, LANES)
    pick[:, :pairs] = pick_f[:, :pairs].astype(BF16)
    pick[:, pairs:] = pick_f[:, :pairs].astype(BF16)
    pick_t[...] = pick_tf[:pairs, :].astype(BF16)
    hot_slab = jnp.where((slab_row == sub.astype(F32)) & live_row, 1.0, 0.0)
    hot_slab_t = hot_slab.T
    sums_by_slab[:, :pairs] = hot_slab[:slabs, :pairs].astype(BF16)
    sums_by_slab[:, pairs:] = hot_slab[:slabs, :pairs].astype(BF16)
    slab_hot_t[:, :slabs] = hot_slab_t[:pairs, :slabs].astype(BF16)
    slab_hot_t[:, slabs:] = hot_slab_t[:pairs, :slabs].astype(BF16)

    wide = (half, LANES)
    low_lane = iota(wide, 1) < BLOCK

    def to_rows(source, target):
        for r in range(half):
            cols = pl.ds(r * LANES, LANES)
            flat[pl.ds(r, 8, stride=half), :] = source[0:8, cols]
            flat[8 * half + r : 8 * half + r + 1, :] = source[8:9, cols]
        for i in range(5):
            left = flat[pl.ds(2 * i * half, half), :]
            if i < 4:
                right = flat[pl.ds((2 * i + 1) * half, half), :]
            else:
                right = jnp.zeros(wide, F32)
            cols = pl.ds(i * LANES, LANES)
            target[0:half, cols] = jnp.where(low_lane, left, pltpu.roll(right, BLOCK, 1))
            target[half:, cols] = jnp.where(low_lane, pltpu.roll(left, BLOCK, 1), right)

    def from_rows(value, target):
        for i in range(5):
            even = value[0:half, i * LANES : (i + 1) * LANES]
            odd = value[half:, i * LANES : (i + 1) * LANES]
            flat[pl.ds(2 * i * half, half), :] = jnp.where(low_lane, even, pltpu.roll(odd, BLOCK, 1))
            if i < 4:
                flat[pl.ds((2 * i + 1) * half, half), :] = jnp.where(
                    low_lane, pltpu.roll(even, BLOCK, 1), odd
                )
        for r in range(half):
            cols = pl.ds(r * LANES, LANES)
            target[0:8, cols] = flat[pl.ds(r, 8, stride=half), :]
            target[8:9, cols] = flat[8 * half + r : 8 * half + r + 1, :]

    to_rows(rs_ref, v0)
    to_rows(damp_ref, damp)

    pl.semaphore_wait(barrier, owners + ncam - 2)

    def pt_exchange(sources, target, send_sem, recv_sem):
        copies = []
        for hop in range(1, owners):
            peer = lax.rem(me_pt + hop, owners)
            copy = pltpu.make_async_remote_copy(
                src_ref=sources(peer), dst_ref=target.at[me_pt],
                send_sem=send_sem.at[hop - 1], recv_sem=recv_sem.at[hop - 1],
                device_id=at_pt(peer), device_id_type=MESH,
            )
            copy.start()
            copies.append(copy)
        return copies

    def wait_all(copies):
        for copy in copies:
            copy.wait()

    ask_copies = pt_exchange(lambda peer: asks_mine.at[peer], asks, ask_send, ask_recv)
    asks[me_pt] = asks_mine[me_pt]

    def to_sibling(source, target, sems, c):
        copy = pltpu.make_async_remote_copy(
            src_ref=source, dst_ref=target, send_sem=sems.at[0, c], recv_sem=sems.at[1, c],
            device_id=at_cam(sibling), device_id_type=MESH,
        )
        copy.start()
        return [copy]

    def to_far(source, target, sems, c):
        copies = []
        for hop in range(1, nx):
            peer = far(hop)
            copy = pltpu.make_async_remote_copy(
                src_ref=source(peer), dst_ref=target(hop),
                send_sem=sems.at[0, c, hop - 1], recv_sem=sems.at[1, c, hop - 1],
                device_id=at_cam(peer * 2 + me_core), device_id_type=MESH,
            )
            copy.start()
            copies.append(copy)
        return copies

    def put_parts(buf, c, k, value):
        for q in range(ncam):
            buf[c, q % 2, q // 2, k] = value[:, q * part : (q + 1) * part]

    loads[0].wait()
    h_copies = []
    for c in range(CHUNKS):

        def hess_tile(t, carry, c=c):
            col = pl.multiple_of(c * width + t * LANES, LANES)
            spot = pl.ds(pl.multiple_of(t * LANES, LANES), LANES)
            for g in range(pairs // 16):
                rows = slice(g * 16, g * 16 + 16)
                point = [jp[k, rows, pl.ds(col, LANES)].astype(F32) for k in range(6)]
                for f, (a, b) in enumerate(HESS):
                    high, low = split2(point[a] * point[b] + point[3 + a] * point[3 + b])
                    tbuf[f, rows, spot] = high
                    tbuf[f, pairs + g * 16 : pairs + g * 16 + 16, spot] = low
            return carry

        lax.fori_loop(0, width // LANES, hess_tile, 0)
        for f in range(6):
            put_parts(h_part, c, f, dot(sums_by_slab[...], tbuf[f]))
        h_copies.append(to_sibling(h_part.at[c, 1 - me_core], h_sib.at[c], hs_sem, c))

    wait_all(ask_copies)
    wanted = asks[...].reshape(spots, LANES)
    hot = jnp.where(wanted == lane.astype(F32), 1.0, 0.0)
    place[...] = hot[:, : 2 * half].astype(BF16)
    place_t[...] = hot.T[: 2 * half, :].astype(BF16)

    def send_blocks(vec, it):
        out = select_rows(place[...], vec[...])
        packed[it] = out.reshape(owners, cap, COLS)
        got[it, me_pt] = packed[it, me_pt]
        return pt_exchange(
            lambda peer: packed.at[it, peer], got.at[it], a_send.at[it], a_recv.at[it]
        )

    def make_tables(it):
        value = select_rows(pick_t[...], got[it].reshape(spots, COLS))
        for i in range(5):
            tables[i] = value[:, i * LANES : (i + 1) * LANES]

    a_copies = send_blocks(v0, 0)

    h_far_copies = []
    for c in range(CHUNKS):
        wait_all(h_copies[c])
        h_red[c] = h_part[c, me_core] + h_sib[c]
        h_far_copies.append(
            to_far(lambda peer: h_red.at[c, peer], lambda hop: h_far.at[c, hop - 1], hx_sem, c)
        )

    def finish_hessian(c):
        wait_all(h_far_copies[c])
        for t in range(part // LANES):
            cols = pl.ds(t * LANES, LANES)
            hess = []
            for f in range(6):
                total = h_red[c, me_x, f, :, cols]
                for hop in range(1, nx):
                    total = total + h_far[c, hop - 1, f, :, cols]
                hess.append(total)
            tile = (c * width + me_cam * part) // LANES + t
            damping = pdamp_ref[pl.ds(tile, slabs, stride=row_tiles), :]
            for f, value in enumerate(invert(hess, damping)):
                inverse[c, f, :, cols] = value

    def forward(c, it):
        def tile(t, carry):
            col = pl.multiple_of(c * width + t * LANES, LANES)
            cols = pl.ds(col, LANES)
            spot = pl.ds(pl.multiple_of(t * LANES, LANES), LANES)
            for g in range(pairs // 16):
                rows = slice(g * 16, g * 16 + 16)
                index = [idx[rows, cols]]
                index.append(index[0] + BLOCK)
                pr = [None, None]
                for k in range(9):
                    at_camera = jnp.take_along_axis(
                        tables[k // 2, rows, :], index[k % 2], axis=1, mode="promise_in_bounds"
                    )
                    for i in range(2):
                        term = jc[9 * i + k, rows, cols].astype(F32) * at_camera
                        pr[i] = term if k == 0 else pr[i] + term
                for i in range(2):
                    proj[i, rows, cols] = pr[i]
                for f in range(3):
                    made = (
                        jp[f, rows, cols].astype(F32) * pr[0]
                        + jp[3 + f, rows, cols].astype(F32) * pr[1]
                    )
                    high, low = split2(made)
                    tbuf[f, rows, spot] = high
                    tbuf[f, pairs + g * 16 : pairs + g * 16 + 16, spot] = low
            return carry

        lax.fori_loop(0, width // LANES, tile, 0)
        for f in range(3):
            put_parts(y_part.at[it], c, f, dot(sums_by_slab[...], tbuf[f]))
        return to_sibling(
            y_part.at[it, c, 1 - me_core], y_sib.at[it, c], ys_sem.at[it], c
        )

    def reduce_sibling(c, it, copies):
        wait_all(copies)
        y_red[it, c] = y_part[it, c, me_core] + y_sib[it, c]
        return to_far(
            lambda peer: y_red.at[it, c, peer],
            lambda hop: y_far.at[it, c, hop - 1],
            yx_sem.at[it], c,
        )

    def eliminate(c, it, copies):
        if it == 0:
            finish_hessian(c)
        wait_all(copies)
        vec = []
        for f in range(3):
            total = y_red[it, c, me_x, f]
            for hop in range(1, nx):
                total = total + y_far[it, c, hop - 1, f]
            vec.append(total)
        for f, value in enumerate(apply_inverse([inverse[c, f] for f in range(6)], vec)):
            z_all[it, c, me_core, me_x, f] = value
        here = z_all.at[it, c, me_core, me_x]
        return to_far(lambda peer: here, lambda hop: here, zx_sem.at[it], c)

    def share(c, it, copies):
        wait_all(copies)
        here = z_all.at[it, c, me_core]
        return to_sibling(here, here, zs_sem.at[it], c)

    def backward(c, it, copies):
        wait_all(copies)
        for q in range(ncam):
            for f in range(3):
                high, low = split2(z_all[it, c, q % 2, q // 2, f])
                zslot[f, :, q * part : (q + 1) * part] = dot(
                    slab_hot_t[...], jnp.concatenate([high, low], axis=0)
                )

        def group(g, carry):
            base = pl.multiple_of(g * 16, 16)
            rows = pl.ds(base, 16)
            for t in range(width // LANES):
                cols = pl.ds(c * width + t * LANES, LANES)
                spot = pl.ds(t * LANES, LANES)
                miss = [proj[i, rows, cols] for i in range(2)]
                for f in range(3):
                    z = zslot[f, rows, spot]
                    for i in range(2):
                        miss[i] = miss[i] - jp[3 * i + f, rows, cols].astype(F32) * z
                push = [
                    jc[k, rows, cols].astype(F32) * miss[0]
                    + jc[9 + k, rows, cols].astype(F32) * miss[1]
                    for k in range(9)
                ]
                for h in range(2):
                    mine = [value[h * 8 : h * 8 + 8] for value in push]
                    last_high = mine[8].astype(BF16).astype(F32)
                    for i in range(4):
                        pair = jnp.concatenate([mine[2 * i], mine[2 * i + 1]], axis=0)
                        high, low = split2(pair)
                        pbuf[h, 16 * i : 16 * i + 16, spot] = high
                        pbuf[h, 80 + 16 * i : 96 + 16 * i, spot] = low
                    pair = jnp.concatenate([last_high, mine[8] - last_high], axis=0)
                    pbuf[h, 64:80, spot] = pair.astype(BF16)
            cams = iota((BLOCK, 2 * LANES), 0)
            for h in range(2):
                for s in range(2):
                    total = None
                    for t in range(width // (2 * LANES)):
                        cols = pl.ds(c * width + t * 2 * LANES, 2 * LANES)
                        here = idx[pl.ds(pl.multiple_of(base + h * 8, 8), 8), cols]
                        hots = []
                        for j in range(4):
                            line = here[s * 4 + j : s * 4 + j + 1, :]
                            line = jnp.broadcast_to(line, (BLOCK, 2 * LANES))
                            hots.append(jnp.where(cams == line, 1.0, 0.0).astype(BF16))
                        piece = lax.dot_general(
                            pbuf[h, :, t * 2 * LANES : (t + 1) * 2 * LANES],
                            jnp.concatenate(hots, axis=0),
                            (((1,), (1,)), ((), ())),
                            preferred_element_type=F32,
                        )
                        total = piece if total is None else total + piece
                    if c == 0:
                        acc[2 * g + h, s] = total
                    else:
                        acc[2 * g + h, s] += total
            return carry

        lax.fori_loop(0, pairs // 16, group, 0)

    def slot_sums():
        small = (8, LANES)
        row = iota(small, 0)
        first4 = row < 4
        right = lax.rem(row, 4) >= 2
        odd = lax.rem(row, 2) == 1
        low8 = iota(small, 1) < BLOCK

        def one(g, carry):
            lows, highs = [], []
            for f in range(9):
                other = 72 if f == 8 else 80 + 8 * f
                cut = []
                for s in range(2):
                    cut.append(acc[g, s, 8 * f : 8 * f + 8, :] + acc[g, s, other : other + 8, :])
                here = jnp.where(
                    right,
                    jnp.where(first4, cut[0][:, LANES:], cut[1][:, LANES:]),
                    jnp.where(first4, cut[0][:, :LANES], cut[1][:, :LANES]),
                )
                turned = pltpu.roll(here, BLOCK, 1)
                lows.append(jnp.where(odd, turned, here))
                highs.append(jnp.where(odd, here, turned))
            rows = pl.ds(pl.multiple_of(g * 8, 8), 8)
            for i in range(5):
                high = highs[2 * i + 1] if i < 4 else jnp.zeros(small, F32)
                slotsum[rows, i * LANES : (i + 1) * LANES] = jnp.where(low8, lows[2 * i], high)
            return carry

        lax.fori_loop(0, pairs // 8, one, 0)

    def schur(vec, it, a_copies, beside):
        wait_all(a_copies)
        make_tables(it)
        next(beside, None)
        if it == 0:
            loads[1].wait()
            loads[2].wait()
        first, second, third, fourth = {}, {}, {}, {}
        for step in range(CHUNKS + 3):
            if step < CHUNKS:
                first[step] = forward(step, it)
                next(beside, None)
            if 0 <= step - 1 < CHUNKS:
                second[step - 1] = reduce_sibling(step - 1, it, first[step - 1])
            if 0 <= step - 2 < CHUNKS:
                third[step - 2] = eliminate(step - 2, it, second[step - 2])
            if 0 <= step - 3 < CHUNKS:
                fourth[step - 3] = share(step - 3, it, third[step - 3])
            if step - 3 >= 0 and step >= CHUNKS - 1:
                backward(step - 3, it, fourth[step - 3])
        slot_sums()
        next(beside, None)
        high, low = split2(slotsum[...])
        out = dot(pick[...], jnp.concatenate([high, low], axis=0))
        out_pack[it] = out.reshape(owners, cap, COLS)
        in_pack[it, me_pt] = out_pack[it, me_pt]
        copies = pt_exchange(
            lambda peer: out_pack.at[it, peer], in_pack.at[it], e_send.at[it], e_recv.at[it]
        )
        wait_all(copies)
        high, low = split2(in_pack[it].reshape(spots, COLS))
        total = dot(place_t[...], high) + dot(place_t[...], low)
        return damp[...] * vec[...] + total

    def fill(value):
        return jnp.broadcast_to(jnp.sum(value, keepdims=True), (8, LANES))

    def start_dots(values, n):
        for k, value in enumerate(values):
            dots[n, k] = fill(value)
        copies = []
        for hop in range(1, owners):
            copy = pltpu.make_async_remote_copy(
                src_ref=dots.at[n], dst_ref=dots_pt.at[n, hop - 1],
                send_sem=dp_sem.at[0, n, hop - 1], recv_sem=dp_sem.at[1, n, hop - 1],
                device_id=at_pt(lax.rem(me_pt + hop, owners)), device_id_type=MESH,
            )
            copy.start()
            copies.append(copy)
        return copies

    def pass_dots(copies, n):
        wait_all(copies)
        total = dots[n]
        for hop in range(1, owners):
            total = total + dots_pt[n, hop - 1]
        dots_cam[n, 0] = total
        copies = []
        for hop in range(1, ncam):
            copy = pltpu.make_async_remote_copy(
                src_ref=dots_cam.at[n, 0], dst_ref=dots_cam.at[n, hop],
                send_sem=dc_sem.at[0, n, hop - 1], recv_sem=dc_sem.at[1, n, hop - 1],
                device_id=at_cam(lax.rem(me_cam + hop, ncam)), device_id_type=MESH,
            )
            copy.start()
            copies.append(copy)
        return copies

    def end_dots(copies, n, k):
        wait_all(copies)
        total = dots_cam[n, 0]
        for hop in range(1, ncam):
            total = total + dots_cam[n, hop]
        return [total[i][0:1, 0:1] for i in range(k)]

    v1[...] = schur(v0, 0, a_copies, iter(()))
    a_copies = send_blocks(v1, 1)
    known = []

    def scalars(copies):
        copies = pass_dots(copies, 0)
        yield
        yield
        norm0, curve0 = end_dots(copies, 0, 2)
        step0 = norm0 / curve0
        res1 = v0[...] - step0 * v1[...]
        copies = start_dots([res1 * res1], 1)
        yield
        yield
        copies = pass_dots(copies, 1)
        yield
        (norm1,) = end_dots(copies, 1, 1)
        known.extend([norm0, norm1, step0])
        yield

    copies = start_dots([v0[...] * v0[...], v0[...] * v1[...]], 0)
    v2[...] = schur(v1, 1, a_copies, scalars(copies))
    norm0, norm1, step0 = known
    res1 = v0[...] - step0 * v1[...]
    ratio = norm1 / norm0
    dir1 = res1 + ratio * v0[...]
    image1 = v1[...] - step0 * v2[...] + ratio * v1[...]
    three = start_dots([dir1 * image1], 2)
    three = pass_dots(three, 2)
    (curve1,) = end_dots(three, 2, 1)
    step1 = norm1 / curve1
    from_rows(step0 * v0[...] + step1 * dir1, answer_ref)
    from_rows(res1 - step1 * image1, residual_ref)


def per_device(
    right_side, cam_damping, point_damping, block_ids, slab_ids, cam_index, cam_jacobian,
    point_jacobian, pair_count,
):
    pairs = block_ids.shape[2]
    points = cam_index.shape[3]
    slabs = point_damping.shape[0] // points
    cam_dev = right_side.shape[1]
    blocks_dev = cam_dev // BLOCK
    owners = lax.axis_size("pt")
    ncam = lax.axis_size("cam")
    nx = ncam // 2
    spots = 2 * pairs
    cap = spots // owners
    width = points // CHUNKS
    part = width // ncam
    idx = cam_index.reshape(pairs, points)
    jc = cam_jacobian.reshape(pairs, 18, points).transpose(1, 0, 2)
    jp = point_jacobian.reshape(pairs, 6, points).transpose(1, 0, 2)
    vmem = pl.BlockSpec(memory_space=pltpu.VMEM)
    hbm = pl.BlockSpec(memory_space=pl.ANY)
    V = pltpu.VMEM
    D = pltpu.SemaphoreType.DMA
    far = max(nx - 1, 1)
    scratch = [
        V((pairs, points), jnp.int32), V((18, pairs, points), BF16), V((6, pairs, points), BF16),
        D((3,)),
        V((spots, blocks_dev), BF16), V((blocks_dev, spots), BF16),
        V((spots, 2 * pairs), BF16), V((pairs, spots), BF16),
        V((slabs, 2 * pairs), BF16), V((pairs, 2 * slabs), BF16),
        V((owners, cap, LANES), F32), V((owners, cap, LANES), F32),
        V((9 * blocks_dev // 2, LANES), F32),
        V((blocks_dev, COLS), F32), V((blocks_dev, COLS), F32), V((blocks_dev, COLS), F32),
        V((blocks_dev, COLS), F32),
        V((ITERS, owners, cap, COLS), F32), V((ITERS, owners, cap, COLS), F32),
        V((5, pairs, LANES), F32),
        V((2, pairs, points), F32),
        V((6, 2 * pairs, width), BF16),
        V((3, pairs, width), F32),
        V((2, 144, width), BF16),
        V((pairs // 8, 2, 144, 4 * BLOCK), F32),
        V((pairs, COLS), F32),
        V((CHUNKS, 2, nx, 6, slabs, part), F32), V((CHUNKS, nx, 6, slabs, part), F32),
        V((CHUNKS, nx, 6, slabs, part), F32), V((CHUNKS, far, 6, slabs, part), F32),
        V((CHUNKS, 6, slabs, part), F32),
        V((ITERS, CHUNKS, 2, nx, 3, slabs, part), F32), V((ITERS, CHUNKS, nx, 3, slabs, part), F32),
        V((ITERS, CHUNKS, nx, 3, slabs, part), F32), V((ITERS, CHUNKS, far, 3, slabs, part), F32),
        V((ITERS, CHUNKS, 2, nx, 3, slabs, part), F32),
        V((ITERS, owners, cap, COLS), F32), V((ITERS, owners, cap, COLS), F32),
        V((3, 2, 8, LANES), F32), V((3, owners - 1, 2, 8, LANES), F32),
        V((3, ncam, 2, 8, LANES), F32),
        D((owners - 1,)), D((owners - 1,)),
        D((ITERS, owners - 1)), D((ITERS, owners - 1)),
        D((ITERS, owners - 1)), D((ITERS, owners - 1)),
        D((2, CHUNKS)), D((2, CHUNKS, far)),
        D((ITERS, 2, CHUNKS)), D((ITERS, 2, CHUNKS, far)),
        D((ITERS, 2, CHUNKS, far)), D((ITERS, 2, CHUNKS)),
        D((2, 3, owners - 1)), D((2, 3, ncam - 1)),
    ]
    return pl.pallas_call(
        body,
        name="cg",
        out_shape=[jax.ShapeDtypeStruct((9, cam_dev), F32)] * 2,
        in_specs=[vmem] * 6 + [hbm] * 3,
        out_specs=[vmem] * 2,
        scratch_shapes=scratch,
        compiler_params=pltpu.CompilerParams(
            collective_id=0, has_side_effects=True, vmem_limit_bytes=VMEM_BYTES
        ),
    )(
        block_ids.reshape(1, pairs), slab_ids.reshape(1, pairs), pair_count.reshape(1, 1),
        right_side, cam_damping, point_damping.reshape(-1, LANES), idx, jc, jp,
    )


def solution(mesh):
    in_specs = (
        P(None, ("cam", "pt")),
        P(None, ("cam", "pt")),
        P("pt"),
        P("cam", "pt", None),
        P("cam", "pt", None),
        P("cam", "pt", None, None),
        P("cam", "pt", None, None, None),
        P("cam", "pt", None, None, None),
        P("cam", "pt"),
    )
    out_specs = (P(None, ("cam", "pt")), P(None, ("cam", "pt")))
    return jax.shard_map(
        per_device, mesh=mesh, in_specs=in_specs, out_specs=out_specs, check_vma=False
    )
```

```python
import functools

import jax
import jax.numpy as jnp
from jax import lax
from jax.experimental import pallas as pl
from jax.experimental.pallas import tpu as pltpu
from jax.sharding import PartitionSpec as P

BLOCK = 64
ITERS = 2
LANES = 128
CHUNKS = 4
COLS = 5 * LANES
KCOLS = 4 * LANES
F32 = jnp.float32
BF16 = jnp.bfloat16
VMEM_BYTES = 60 * 1024 * 1024
MESH = pl.DeviceIdType.MESH
HESS = [(0, 0), (1, 1), (2, 2), (0, 1), (1, 2), (0, 2)]


def iota(shape, axis):
    return lax.broadcasted_iota(jnp.int32, shape, axis)


def split2(value):
    high = value.astype(BF16)
    return high, (value - high.astype(F32)).astype(BF16)


def split3(value):
    high, low = split2(value)
    last = value - high.astype(F32) - low.astype(F32)
    return high, low, last.astype(BF16)


def dot(a, b):
    return jnp.dot(a, b, preferred_element_type=F32)


def select_rows(hot, value):
    parts = split3(value)
    return dot(hot, parts[0]) + dot(hot, parts[1]) + dot(hot, parts[2])


def invert(hess, damping):
    xx, yy, zz = (hess[k] + damping for k in range(3))
    xy, yz, xz = hess[3], hess[4], hess[5]
    cof_xx = yy * zz - yz * yz
    cof_xy = xz * yz - xy * zz
    cof_xz = xy * yz - xz * yy
    cof_yy = xx * zz - xz * xz
    cof_yz = xy * xz - xx * yz
    cof_zz = xx * yy - xy * xy
    det = xx * cof_xx + xy * cof_xy + xz * cof_xz
    return [c / det for c in (cof_xx, cof_xy, cof_xz, cof_yy, cof_yz, cof_zz)]


def apply_inverse(inv, vec):
    return [
        inv[0] * vec[0] + inv[1] * vec[1] + inv[2] * vec[2],
        inv[1] * vec[0] + inv[3] * vec[1] + inv[4] * vec[2],
        inv[2] * vec[0] + inv[4] * vec[1] + inv[5] * vec[2],
    ]


def body(
    ids_ref, slab_ref, count_ref, rs_ref, damp_ref, pdamp_ref, idx_hbm, jc_hbm, jp_hbm,
    answer_ref, residual_ref,
    idx, jc, jp, hots, load_sem,
    place, place_t, pick, pick_t, sums_by_slab, slab_hot_t, asks_mine, asks,
    flat, v0, v1, v2, damp, packed, got, tables, proj, tbuf, zslot, pbuf, acc, slotsum,
    h_part, h_sib, h_red, h_far, inverse, y_part, y_sib, y_red, y_far, z_all,
    out_pack, in_pack, dots, dots_pt, dots_cam,
    ask_send, ask_recv, a_send, a_recv, e_send, e_recv,
    hs_sem, hx_sem, ys_sem, yx_sem, zx_sem, zs_sem, dp_sem, dc_sem,
):
    pairs, points = idx.shape
    owners = lax.axis_size("pt")
    ncam = lax.axis_size("cam")
    nx = ncam // 2
    me_pt = lax.axis_index("pt")
    me_cam = lax.axis_index("cam")
    me_x = me_cam // 2
    me_core = lax.rem(me_cam, 2)
    sibling = me_x * 2 + (1 - me_core)
    spots = 2 * pairs
    cap = spots // owners
    slabs = sums_by_slab.shape[0]
    width = points // CHUNKS
    part = width // ncam
    half = v0.shape[0] // 2
    row_tiles = points // LANES

    def far(hop):
        return lax.rem(me_x + hop, nx)

    def at_cam(cam):
        return {"cam": cam}

    def at_pt(pt):
        return {"pt": pt}

    loads = [
        pltpu.make_async_copy(jp_hbm, jp, load_sem.at[0]),
        pltpu.make_async_copy(idx_hbm, idx, load_sem.at[1]),
        pltpu.make_async_copy(jc_hbm, jc, load_sem.at[2]),
    ]
    for copy in loads:
        copy.start()

    barrier = pltpu.get_barrier_semaphore()
    for hop in range(1, owners):
        pl.semaphore_signal(
            barrier, inc=1, device_id=at_pt(lax.rem(me_pt + hop, owners)), device_id_type=MESH
        )
    for hop in range(1, ncam):
        pl.semaphore_signal(
            barrier, inc=1, device_id=at_cam(lax.rem(me_cam + hop, ncam)), device_id_type=MESH
        )

    square = (LANES, LANES)
    sub, lane = iota(square, 0), iota(square, 1)
    blank = jnp.zeros((1, LANES - pairs), F32)
    ids_row = jnp.concatenate([ids_ref[...].astype(F32), blank], axis=1)
    slab_row = jnp.concatenate([slab_ref[...].astype(F32), blank], axis=1)
    count = jnp.broadcast_to(count_ref[...], square)
    live_row = lane < count
    live_col = sub < count
    ids_row = jnp.broadcast_to(ids_row, square).astype(jnp.int32)
    slab_row = jnp.broadcast_to(slab_row, square)
    ids_col = ids_row.astype(F32).T.astype(jnp.int32)
    blocks_dev = 2 * half
    owner_row = ids_row // blocks_dev
    owner_col = ids_col // blocks_dev
    same = jnp.where(owner_row == owner_col, 1.0, 0.0)
    before = jnp.where((lane < sub) & live_row, same, 0.0)
    rank_col = jnp.broadcast_to(jnp.sum(before, axis=1, keepdims=True), square)
    pos_col = owner_col * cap + rank_col.astype(jnp.int32)
    pos_row = pos_col.astype(F32).T.astype(jnp.int32)
    pick_f = jnp.where((pos_row == sub) & live_row, 1.0, 0.0)
    pick_tf = jnp.where((pos_col == lane) & live_col, 1.0, 0.0)
    local = ids_row - owner_row * blocks_dev
    local = local // 2 + half * (local - (local // 2) * 2)
    asked = jnp.sum(pick_f * (local + 1).astype(F32), axis=1, keepdims=True) - 1.0
    asks_mine[...] = jnp.broadcast_to(asked, square).reshape(owners, cap, LANES)
    pick[:, :pairs] = pick_f[:, :pairs].astype(BF16)
    pick[:, pairs:] = pick_f[:, :pairs].astype(BF16)
    pick_t[...] = pick_tf[:pairs, :].astype(BF16)
    hot_slab = jnp.where((slab_row == sub.astype(F32)) & live_row, 1.0, 0.0)
    hot_slab_t = hot_slab.T
    sums_by_slab[:, :pairs] = hot_slab[:slabs, :pairs].astype(BF16)
    sums_by_slab[:, pairs:] = hot_slab[:slabs, :pairs].astype(BF16)
    slab_hot_t[:, :slabs] = hot_slab_t[:pairs, :slabs].astype(BF16)
    slab_hot_t[:, slabs:] = hot_slab_t[:pairs, :slabs].astype(BF16)

    wide = (half, LANES)
    low_lane = iota(wide, 1) < BLOCK

    def to_rows(source, target):
        for r in range(half):
            cols = pl.ds(r * LANES, LANES)
            flat[pl.ds(r, 8, stride=half), :] = source[0:8, cols]
            flat[8 * half + r : 8 * half + r + 1, :] = source[8:9, cols]
        for i in range(5):
            left = flat[pl.ds(2 * i * half, half), :]
            if i < 4:
                right = flat[pl.ds((2 * i + 1) * half, half), :]
            else:
                right = jnp.zeros(wide, F32)
            cols = pl.ds(i * LANES, LANES)
            target[0:half, cols] = jnp.where(low_lane, left, pltpu.roll(right, BLOCK, 1))
            target[half:, cols] = jnp.where(low_lane, pltpu.roll(left, BLOCK, 1), right)

    def from_rows(value, target):
        for i in range(5):
            even = value[0:half, i * LANES : (i + 1) * LANES]
            odd = value[half:, i * LANES : (i + 1) * LANES]
            target[2 * i] = jnp.where(low_lane, even, pltpu.roll(odd, BLOCK, 1))
            if i < 4:
                target[2 * i + 1] = jnp.where(low_lane, pltpu.roll(even, BLOCK, 1), odd)

    to_rows(rs_ref, v0)
    to_rows(damp_ref, damp)

    pl.semaphore_wait(barrier, owners + ncam - 2)

    def pt_exchange(sources, target, send_sem, recv_sem):
        copies = []
        for hop in range(1, owners):
            peer = lax.rem(me_pt + hop, owners)
            copy = pltpu.make_async_remote_copy(
                src_ref=sources(peer), dst_ref=target.at[me_pt],
                send_sem=send_sem.at[hop - 1], recv_sem=recv_sem.at[hop - 1],
                device_id=at_pt(peer), device_id_type=MESH,
            )
            copy.start()
            copies.append(copy)
        return copies

    def wait_all(copies):
        for copy in copies:
            copy.wait()

    ask_copies = pt_exchange(lambda peer: asks_mine.at[peer], asks, ask_send, ask_recv)
    asks[me_pt] = asks_mine[me_pt]

    def to_sibling(source, target, sems, c):
        copy = pltpu.make_async_remote_copy(
            src_ref=source, dst_ref=target, send_sem=sems.at[0, c], recv_sem=sems.at[1, c],
            device_id=at_cam(sibling), device_id_type=MESH,
        )
        copy.start()
        return [copy]

    def to_far(source, target, sems, c):
        copies = []
        for hop in range(1, nx):
            peer = far(hop)
            copy = pltpu.make_async_remote_copy(
                src_ref=source(peer), dst_ref=target(hop),
                send_sem=sems.at[0, c, hop - 1], recv_sem=sems.at[1, c, hop - 1],
                device_id=at_cam(peer * 2 + me_core), device_id_type=MESH,
            )
            copy.start()
            copies.append(copy)
        return copies

    def put_parts(buf, c, k, value):
        for q in range(ncam):
            buf[c, q % 2, q // 2, k] = value[:, q * part : (q + 1) * part]

    loads[0].wait()
    h_copies = []
    for c in range(CHUNKS):

        def hess_tile(t, carry, c=c):
            col = pl.multiple_of(c * width + t * LANES, LANES)
            spot = pl.ds(pl.multiple_of(t * LANES, LANES), LANES)
            for g in range(pairs // 16):
                rows = slice(g * 16, g * 16 + 16)
                point = [jp[k, rows, pl.ds(col, LANES)].astype(F32) for k in range(6)]
                for f, (a, b) in enumerate(HESS):
                    high, low = split2(point[a] * point[b] + point[3 + a] * point[3 + b])
                    tbuf[f, rows, spot] = high
                    tbuf[f, pairs + g * 16 : pairs + g * 16 + 16, spot] = low
            return carry

        lax.fori_loop(0, width // LANES, hess_tile, 0)
        for f in range(6):
            put_parts(h_part, c, f, dot(sums_by_slab[...], tbuf[f]))
        h_copies.append(to_sibling(h_part.at[c, 1 - me_core], h_sib.at[c], hs_sem, c))

    wait_all(ask_copies)
    wanted = asks[...].reshape(spots, LANES)
    hot = jnp.where(wanted == lane.astype(F32), 1.0, 0.0)
    place[...] = hot[:, : 2 * half].astype(BF16)
    place_t[...] = hot.T[: 2 * half, :].astype(BF16)

    short_low = iota((cap // 2, LANES), 1) < BLOCK

    def pack(value, buf):
        for o in range(owners):
            rows = value[o * cap : (o + 1) * cap]
            for i in range(4):
                buf[o, i * cap : (i + 1) * cap, :] = rows[:, i * LANES : (i + 1) * LANES]
            last = rows[:, 4 * LANES :]
            buf[o, 4 * cap :, :] = jnp.where(
                short_low, last[: cap // 2], pltpu.roll(last[cap // 2 :], BLOCK, 1)
            )

    def unpack(buf):
        tall = []
        for o in range(owners):
            cols = [buf[o, i * cap : (i + 1) * cap, :] for i in range(4)]
            last = buf[o, 4 * cap :, :]
            zero = jnp.zeros_like(last)
            last = [
                jnp.where(short_low, last, zero),
                jnp.where(short_low, pltpu.roll(last, BLOCK, 1), zero),
            ]
            cols.append(jnp.concatenate(last, axis=0))
            tall.append(jnp.concatenate(cols, axis=1))
        return jnp.concatenate(tall, axis=0)

    def send_blocks(vec, it):
        pack(select_rows(place[...], vec[...]), packed.at[it])
        got[it, me_pt] = packed[it, me_pt]
        return pt_exchange(
            lambda peer: packed.at[it, peer], got.at[it], a_send.at[it], a_recv.at[it]
        )

    def make_tables(it):
        value = select_rows(pick_t[...], unpack(got.at[it]))
        for i in range(5):
            here = value[:, i * LANES : (i + 1) * LANES]
            tables[2 * i] = here
            if i < 4:
                tables[2 * i + 1] = pltpu.roll(here, BLOCK, 1)

    a_copies = send_blocks(v0, 0)

    loads[1].wait()

    def hot_tile(t, carry):
        cols = pl.ds(pl.multiple_of(t * LANES, LANES), LANES)
        cams = iota((BLOCK // 2, LANES), 0)
        here = idx[:, cols] & (BLOCK // 2 - 1)
        for j in range(pairs):
            line = jnp.broadcast_to(here[j : j + 1, :], (BLOCK // 2, LANES))
            hots[j * BLOCK // 2 : (j + 1) * BLOCK // 2, cols] = jnp.where(
                cams == line, 1.0, 0.0
            ).astype(BF16)
        return carry

    lax.fori_loop(0, points // LANES, hot_tile, 0)

    h_far_copies = []
    for c in range(CHUNKS):
        wait_all(h_copies[c])
        h_red[c] = h_part[c, me_core] + h_sib[c]
        h_far_copies.append(
            to_far(lambda peer: h_red.at[c, peer], lambda hop: h_far.at[c, hop - 1], hx_sem, c)
        )

    def finish_hessian(c):
        wait_all(h_far_copies[c])
        for t in range(part // LANES):
            cols = pl.ds(t * LANES, LANES)
            hess = []
            for f in range(6):
                total = h_red[c, me_x, f, :, cols]
                for hop in range(1, nx):
                    total = total + h_far[c, hop - 1, f, :, cols]
                hess.append(total)
            tile = (c * width + me_cam * part) // LANES + t
            damping = pdamp_ref[pl.ds(tile, slabs, stride=row_tiles), :]
            for f, value in enumerate(invert(hess, damping)):
                inverse[c, f, :, cols] = value

    def forward(c, it):
        def tile(t, carry):
            col = pl.multiple_of(c * width + t * LANES, LANES)
            cols = pl.ds(col, LANES)
            spot = pl.ds(pl.multiple_of(t * LANES, LANES), LANES)
            for g in range(pairs // 16):
                rows = slice(g * 16, g * 16 + 16)
                index = idx[rows, cols]
                pr = [None, None]
                for k in range(9):
                    at_camera = jnp.take_along_axis(
                        tables[k, rows, :], index, axis=1, mode="promise_in_bounds"
                    )
                    for i in range(2):
                        term = jc[9 * i + k, rows, cols].astype(F32) * at_camera
                        pr[i] = term if k == 0 else pr[i] + term
                for i in range(2):
                    proj[i, rows, cols] = pr[i]
                for f in range(3):
                    made = (
                        jp[f, rows, cols].astype(F32) * pr[0]
                        + jp[3 + f, rows, cols].astype(F32) * pr[1]
                    )
                    high, low = split2(made)
                    tbuf[f, rows, spot] = high
                    tbuf[f, pairs + g * 16 : pairs + g * 16 + 16, spot] = low
            return carry

        lax.fori_loop(0, width // LANES, tile, 0)
        for f in range(3):
            put_parts(y_part.at[it], c, f, dot(sums_by_slab[...], tbuf[f]))
        return to_sibling(
            y_part.at[it, c, 1 - me_core], y_sib.at[it, c], ys_sem.at[it], c
        )

    def reduce_sibling(c, it, copies):
        wait_all(copies)
        y_red[it, c] = y_part[it, c, me_core] + y_sib[it, c]
        return to_far(
            lambda peer: y_red.at[it, c, peer],
            lambda hop: y_far.at[it, c, hop - 1],
            yx_sem.at[it], c,
        )

    def eliminate(c, it, copies):
        if it == 0:
            finish_hessian(c)
        wait_all(copies)
        vec = []
        for f in range(3):
            total = y_red[it, c, me_x, f]
            for hop in range(1, nx):
                total = total + y_far[it, c, hop - 1, f]
            vec.append(total)
        for f, value in enumerate(apply_inverse([inverse[c, f] for f in range(6)], vec)):
            z_all[it, c, me_core, me_x, f] = value
        here = z_all.at[it, c, me_core, me_x]
        return to_far(lambda peer: here, lambda hop: here, zx_sem.at[it], c)

    def share(c, it, copies):
        wait_all(copies)
        here = z_all.at[it, c, me_core]
        return to_sibling(here, here, zs_sem.at[it], c)

    def backward(c, it, copies):
        wait_all(copies)
        for q in range(ncam):
            for f in range(3):
                high, low = split2(z_all[it, c, q % 2, q // 2, f])
                zslot[f, :, q * part : (q + 1) * part] = dot(
                    slab_hot_t[...], jnp.concatenate([high, low], axis=0)
                )

        def build(g):
            base = pl.multiple_of(g * 16, 16)
            rows = pl.ds(base, 16)
            for t in range(width // LANES):
                cols = pl.ds(c * width + t * LANES, LANES)
                spot = pl.ds(t * LANES, LANES)
                miss = [proj[i, rows, cols] for i in range(2)]
                for f in range(3):
                    z = zslot[f, rows, spot]
                    for i in range(2):
                        miss[i] = miss[i] - jp[3 * i + f, rows, cols].astype(F32) * z
                push = [
                    jc[k, rows, cols].astype(F32) * miss[0]
                    + jc[9 + k, rows, cols].astype(F32) * miss[1]
                    for k in range(9)
                ]
                upper = jnp.where(idx[rows, cols] >= BLOCK // 2, 1.0, 0.0)
                for h in range(2):
                    mine = [value[h * 8 : h * 8 + 8] for value in push]
                    last_high = mine[8].astype(BF16).astype(F32)
                    halves = upper[h * 8 : h * 8 + 8]
                    halves = jnp.concatenate([halves, halves], axis=0).astype(BF16) > 0.5
                    tiles = [None] * 9
                    for i in range(4):
                        pair = jnp.concatenate([mine[2 * i], mine[2 * i + 1]], axis=0)
                        tiles[i], tiles[5 + i] = split2(pair)
                    pair = jnp.concatenate([last_high, mine[8] - last_high], axis=0)
                    tiles[4] = pair.astype(BF16)
                    for i, value in enumerate(tiles):
                        pbuf[h, 16 * i : 16 * i + 16, spot] = value
                        above = jnp.where(halves, value, jnp.zeros_like(value))
                        pbuf[h, 144 + 16 * i : 160 + 16 * i, spot] = above

        def scatter(g):
            base = g * 16
            for h in range(2):
                total = None
                for t in range(width // KCOLS):
                    cols = pl.ds(c * width + t * KCOLS, KCOLS)
                    hot_rows = pl.ds(pl.multiple_of((base + h * 8) * (BLOCK // 2), 256), 4 * BLOCK)
                    piece = lax.dot_general(
                        pbuf[h, :, t * KCOLS : (t + 1) * KCOLS],
                        hots[hot_rows, cols],
                        (((1,), (1,)), ((), ())),
                        preferred_element_type=F32,
                    )
                    total = piece if total is None else total + piece
                if c == 0:
                    acc[2 * g + h] = total
                else:
                    acc[2 * g + h] += total

        groups = pairs // 16

        def group(g, carry):
            build(g)
            scatter(g)
            return carry

        lax.fori_loop(0, groups, group, 0)

    def slot_sums():
        small = (8, LANES)
        row = iota(small, 0)
        quarter = iota(small, 1) // (BLOCK // 2)
        first4 = row < 4
        turn = lax.rem(row, 4)

        def one(g, carry):
            rows = pl.ds(pl.multiple_of(g * 8, 8), 8)
            for i in range(5):
                line = jnp.zeros(small, F32)
                for q in range(4 if i < 4 else 2):
                    f = 2 * i + q // 2
                    if q % 2 == 0:
                        parts = []
                        for top in (0, 144):
                            low = top + (72 if f == 8 else 80 + 8 * f)
                            parts.append(
                                acc[g, top + 8 * f : top + 8 * f + 8, :] + acc[g, low : low + 8, :]
                            )
                    both = parts[0] - parts[1] if q % 2 == 0 else parts[1]
                    here = jnp.where(first4, both[:, :LANES], both[:, LANES:])
                    moved = None
                    for k in range(4):
                        shift = (32 * (q - k)) % LANES
                        turned = pltpu.roll(here, shift, 1) if shift else here
                        moved = turned if k == 0 else jnp.where(turn == k, turned, moved)
                    line = jnp.where(quarter == q, moved, line)
                slotsum[rows, i * LANES : (i + 1) * LANES] = line
            return carry

        lax.fori_loop(0, pairs // 8, one, 0)

    def schur(vec, it, a_copies, beside):
        wait_all(a_copies)
        make_tables(it)
        next(beside, None)
        if it == 0:
            loads[2].wait()
        first, second, third, fourth = {}, {}, {}, {}
        for step in range(CHUNKS + 4):
            if step < CHUNKS:
                first[step] = forward(step, it)
                next(beside, None)
            if 0 <= step - 1 < CHUNKS:
                second[step - 1] = reduce_sibling(step - 1, it, first[step - 1])
            if 0 <= step - 2 < CHUNKS:
                third[step - 2] = eliminate(step - 2, it, second[step - 2])
            if 0 <= step - 3 < CHUNKS:
                fourth[step - 3] = share(step - 3, it, third[step - 3])
            if step - 4 >= 0:
                backward(step - 4, it, fourth[step - 4])
        slot_sums()
        next(beside, None)
        high, low = split2(slotsum[...])
        pack(dot(pick[...], jnp.concatenate([high, low], axis=0)), out_pack.at[it])
        in_pack[it, me_pt] = out_pack[it, me_pt]
        copies = pt_exchange(
            lambda peer: out_pack.at[it, peer], in_pack.at[it], e_send.at[it], e_recv.at[it]
        )
        wait_all(copies)
        high, low = split2(unpack(in_pack.at[it]))
        total = dot(place_t[...], high) + dot(place_t[...], low)
        return damp[...] * vec[...] + total

    def fill(value):
        return jnp.broadcast_to(jnp.sum(value, keepdims=True), (8, LANES))

    def start_dots(values, n):
        for k, value in enumerate(values):
            dots[n, k] = fill(value)
        copies = []
        for hop in range(1, owners):
            copy = pltpu.make_async_remote_copy(
                src_ref=dots.at[n], dst_ref=dots_pt.at[n, hop - 1],
                send_sem=dp_sem.at[0, n, hop - 1], recv_sem=dp_sem.at[1, n, hop - 1],
                device_id=at_pt(lax.rem(me_pt + hop, owners)), device_id_type=MESH,
            )
            copy.start()
            copies.append(copy)
        return copies

    def pass_dots(copies, n):
        wait_all(copies)
        total = dots[n]
        for hop in range(1, owners):
            total = total + dots_pt[n, hop - 1]
        dots_cam[n, 0] = total
        copies = []
        for hop in range(1, ncam):
            copy = pltpu.make_async_remote_copy(
                src_ref=dots_cam.at[n, 0], dst_ref=dots_cam.at[n, hop],
                send_sem=dc_sem.at[0, n, hop - 1], recv_sem=dc_sem.at[1, n, hop - 1],
                device_id=at_cam(lax.rem(me_cam + hop, ncam)), device_id_type=MESH,
            )
            copy.start()
            copies.append(copy)
        return copies

    def end_dots(copies, n, k):
        wait_all(copies)
        total = dots_cam[n, 0]
        for hop in range(1, ncam):
            total = total + dots_cam[n, hop]
        return [total[i][0:1, 0:1] for i in range(k)]

    v1[...] = schur(v0, 0, a_copies, iter(()))
    a_copies = send_blocks(v1, 1)
    known = []

    def scalars(copies):
        copies = pass_dots(copies, 0)
        yield
        yield
        norm0, curve0 = end_dots(copies, 0, 2)
        step0 = norm0 / curve0
        res1 = v0[...] - step0 * v1[...]
        copies = start_dots([res1 * res1], 1)
        yield
        yield
        copies = pass_dots(copies, 1)
        yield
        (norm1,) = end_dots(copies, 1, 1)
        known.extend([norm0, norm1, step0])
        yield

    copies = start_dots([v0[...] * v0[...], v0[...] * v1[...]], 0)
    v2[...] = schur(v1, 1, a_copies, scalars(copies))
    norm0, norm1, step0 = known
    res1 = v0[...] - step0 * v1[...]
    ratio = norm1 / norm0
    dir1 = res1 + ratio * v0[...]
    image1 = v1[...] - step0 * v2[...] + ratio * v1[...]
    three = start_dots([dir1 * image1], 2)
    three = pass_dots(three, 2)
    (curve1,) = end_dots(three, 2, 1)
    step1 = norm1 / curve1
    from_rows(step0 * v0[...] + step1 * dir1, answer_ref)
    from_rows(res1 - step1 * image1, residual_ref)


def per_device(
    right_side, cam_damping, point_damping, block_ids, slab_ids, cam_index, cam_jacobian,
    point_jacobian, pair_count,
):
    pairs = block_ids.shape[2]
    points = cam_index.shape[3]
    slabs = point_damping.shape[0] // points
    cam_dev = right_side.shape[1]
    blocks_dev = cam_dev // BLOCK
    owners = lax.axis_size("pt")
    ncam = lax.axis_size("cam")
    nx = ncam // 2
    spots = 2 * pairs
    cap = spots // owners
    width = points // CHUNKS
    part = width // ncam
    idx = cam_index.reshape(pairs, points)
    jc = cam_jacobian.reshape(pairs, 18, points).transpose(1, 0, 2)
    jp = point_jacobian.reshape(pairs, 6, points).transpose(1, 0, 2)
    vmem = pl.BlockSpec(memory_space=pltpu.VMEM)
    hbm = pl.BlockSpec(memory_space=pl.ANY)
    V = pltpu.VMEM
    D = pltpu.SemaphoreType.DMA
    far = max(nx - 1, 1)
    scratch = [
        V((pairs, points), jnp.int32), V((18, pairs, points), BF16), V((6, pairs, points), BF16),
        V((pairs * BLOCK // 2, points), BF16),
        D((3,)),
        V((spots, blocks_dev), BF16), V((blocks_dev, spots), BF16),
        V((spots, 2 * pairs), BF16), V((pairs, spots), BF16),
        V((slabs, 2 * pairs), BF16), V((pairs, 2 * slabs), BF16),
        V((owners, cap, LANES), F32), V((owners, cap, LANES), F32),
        V((9 * blocks_dev // 2, LANES), F32),
        V((blocks_dev, COLS), F32), V((blocks_dev, COLS), F32), V((blocks_dev, COLS), F32),
        V((blocks_dev, COLS), F32),
        V((ITERS, owners, 4 * cap + cap // 2, LANES), F32),
        V((ITERS, owners, 4 * cap + cap // 2, LANES), F32),
        V((9, pairs, LANES), F32),
        V((2, pairs, points), F32),
        V((6, 2 * pairs, width), BF16),
        V((3, pairs, width), F32),
        V((2, 288, width), BF16),
        V((pairs // 8, 288, 4 * BLOCK), F32),
        V((pairs, COLS), F32),
        V((CHUNKS, 2, nx, 6, slabs, part), F32), V((CHUNKS, nx, 6, slabs, part), F32),
        V((CHUNKS, nx, 6, slabs, part), F32), V((CHUNKS, far, 6, slabs, part), F32),
        V((CHUNKS, 6, slabs, part), F32),
        V((ITERS, CHUNKS, 2, nx, 3, slabs, part), F32), V((ITERS, CHUNKS, nx, 3, slabs, part), F32),
        V((ITERS, CHUNKS, nx, 3, slabs, part), F32), V((ITERS, CHUNKS, far, 3, slabs, part), F32),
        V((ITERS, CHUNKS, 2, nx, 3, slabs, part), F32),
        V((ITERS, owners, 4 * cap + cap // 2, LANES), F32),
        V((ITERS, owners, 4 * cap + cap // 2, LANES), F32),
        V((3, 2, 8, LANES), F32), V((3, owners - 1, 2, 8, LANES), F32),
        V((3, ncam, 2, 8, LANES), F32),
        D((owners - 1,)), D((owners - 1,)),
        D((ITERS, owners - 1)), D((ITERS, owners - 1)),
        D((ITERS, owners - 1)), D((ITERS, owners - 1)),
        D((2, CHUNKS)), D((2, CHUNKS, far)),
        D((ITERS, 2, CHUNKS)), D((ITERS, 2, CHUNKS, far)),
        D((ITERS, 2, CHUNKS, far)), D((ITERS, 2, CHUNKS)),
        D((2, 3, owners - 1)), D((2, 3, ncam - 1)),
    ]
    outs = pl.pallas_call(
        body,
        name="cg",
        out_shape=[jax.ShapeDtypeStruct((9, blocks_dev // 2, LANES), F32)] * 2,
        in_specs=[vmem] * 6 + [hbm] * 3,
        out_specs=[vmem] * 2,
        scratch_shapes=scratch,
        compiler_params=pltpu.CompilerParams(
            collective_id=0, has_side_effects=True, vmem_limit_bytes=VMEM_BYTES
        ),
    )(
        block_ids.reshape(1, pairs), slab_ids.reshape(1, pairs), pair_count.reshape(1, 1),
        right_side, cam_damping, point_damping.reshape(-1, LANES), idx, jc, jp,
    )
    return outs[0].reshape(9, cam_dev), outs[1].reshape(9, cam_dev)


def solution(mesh):
    in_specs = (
        P(None, ("cam", "pt")),
        P(None, ("cam", "pt")),
        P("pt"),
        P("cam", "pt", None),
        P("cam", "pt", None),
        P("cam", "pt", None, None),
        P("cam", "pt", None, None, None),
        P("cam", "pt", None, None, None),
        P("cam", "pt"),
    )
    out_specs = (P(None, ("cam", "pt")), P(None, ("cam", "pt")))
    return jax.shard_map(
        per_device, mesh=mesh, in_specs=in_specs, out_specs=out_specs, check_vma=False
    )
```

```python
import functools

import jax
import jax.numpy as jnp
from jax import lax
from jax.experimental import pallas as pl
from jax.experimental.pallas import tpu as pltpu
from jax.sharding import PartitionSpec as P

BLOCK = 64
ITERS = 2
LANES = 128
CHUNKS = 4
COLS = 5 * LANES
KCOLS = 4 * LANES
F32 = jnp.float32
BF16 = jnp.bfloat16
VMEM_BYTES = 60 * 1024 * 1024
MESH = pl.DeviceIdType.MESH
HESS = [(0, 0), (1, 1), (2, 2), (0, 1), (1, 2), (0, 2)]


def iota(shape, axis):
    return lax.broadcasted_iota(jnp.int32, shape, axis)


def split2(value):
    high = value.astype(BF16)
    return high, (value - high.astype(F32)).astype(BF16)


def split3(value):
    high, low = split2(value)
    last = value - high.astype(F32) - low.astype(F32)
    return high, low, last.astype(BF16)


def dot(a, b):
    return jnp.dot(a, b, preferred_element_type=F32)


def select_rows(hot, value):
    parts = split3(value)
    return dot(hot, parts[0]) + dot(hot, parts[1]) + dot(hot, parts[2])


def invert(hess, damping):
    xx, yy, zz = (hess[k] + damping for k in range(3))
    xy, yz, xz = hess[3], hess[4], hess[5]
    cof_xx = yy * zz - yz * yz
    cof_xy = xz * yz - xy * zz
    cof_xz = xy * yz - xz * yy
    cof_yy = xx * zz - xz * xz
    cof_yz = xy * xz - xx * yz
    cof_zz = xx * yy - xy * xy
    det = xx * cof_xx + xy * cof_xy + xz * cof_xz
    return [c / det for c in (cof_xx, cof_xy, cof_xz, cof_yy, cof_yz, cof_zz)]


def apply_inverse(inv, vec):
    return [
        inv[0] * vec[0] + inv[1] * vec[1] + inv[2] * vec[2],
        inv[1] * vec[0] + inv[3] * vec[1] + inv[4] * vec[2],
        inv[2] * vec[0] + inv[4] * vec[1] + inv[5] * vec[2],
    ]


def body(
    ids_ref, slab_ref, count_ref, rs_ref, damp_ref, pdamp_ref, idx_hbm, jc_hbm, jp_hbm,
    answer_ref, residual_ref,
    idx, jc, jp, hots, load_sem,
    place, place_t, pick, pick_t, sums_by_slab, slab_hot_t, asks_mine, asks,
    flat, v0, v1, v2, damp, packed, got, tables, proj, tbuf, zslot, pbuf, acc, slotsum,
    h_part, h_sib, h_red, h_far, inverse, y_part, y_sib, y_red, y_far, z_all,
    out_pack, in_pack, dots, dots_pt, dots_cam,
    ask_send, ask_recv, a_send, a_recv, e_send, e_recv,
    hs_sem, hx_sem, ys_sem, yx_sem, zx_sem, zs_sem, dp_sem, dc_sem,
):
    pairs, points = idx.shape
    owners = lax.axis_size("pt")
    ncam = lax.axis_size("cam")
    nx = ncam // 2
    me_pt = lax.axis_index("pt")
    me_cam = lax.axis_index("cam")
    me_x = me_cam // 2
    me_core = lax.rem(me_cam, 2)
    sibling = me_x * 2 + (1 - me_core)
    spots = 2 * pairs
    cap = spots // owners
    slabs = sums_by_slab.shape[0]
    width = points // CHUNKS
    part = width // ncam
    half = v0.shape[0] // 2
    row_tiles = points // LANES

    def far(hop):
        return lax.rem(me_x + hop, nx)

    def at_cam(cam):
        return {"cam": cam}

    def at_pt(pt):
        return {"pt": pt}

    def load(source, target, sem, c):
        cols = pl.ds(c * width, width)
        copy = pltpu.make_async_copy(source.at[:, :, cols], target.at[:, :, cols], sem)
        copy.start()
        return copy

    jp_loads = [load(jp_hbm, jp, load_sem.at[c], c) for c in range(CHUNKS)]
    idx_load = pltpu.make_async_copy(idx_hbm, idx, load_sem.at[2 * CHUNKS])
    idx_load.start()
    jc_loads = [load(jc_hbm, jc, load_sem.at[CHUNKS + c], c) for c in range(CHUNKS)]

    barrier = pltpu.get_barrier_semaphore()
    for hop in range(1, owners):
        pl.semaphore_signal(
            barrier, inc=1, device_id=at_pt(lax.rem(me_pt + hop, owners)), device_id_type=MESH
        )
    for hop in range(1, ncam):
        pl.semaphore_signal(
            barrier, inc=1, device_id=at_cam(lax.rem(me_cam + hop, ncam)), device_id_type=MESH
        )

    square = (LANES, LANES)
    sub, lane = iota(square, 0), iota(square, 1)
    blank = jnp.zeros((1, LANES - pairs), F32)
    ids_row = jnp.concatenate([ids_ref[...].astype(F32), blank], axis=1)
    slab_row = jnp.concatenate([slab_ref[...].astype(F32), blank], axis=1)
    count = jnp.broadcast_to(count_ref[...], square)
    live_row = lane < count
    live_col = sub < count
    ids_row = jnp.broadcast_to(ids_row, square).astype(jnp.int32)
    slab_row = jnp.broadcast_to(slab_row, square)
    ids_col = ids_row.astype(F32).T.astype(jnp.int32)
    blocks_dev = 2 * half
    owner_row = ids_row // blocks_dev
    owner_col = ids_col // blocks_dev
    same = jnp.where(owner_row == owner_col, 1.0, 0.0)
    before = jnp.where((lane < sub) & live_row, same, 0.0)
    rank_col = jnp.broadcast_to(jnp.sum(before, axis=1, keepdims=True), square)
    pos_col = owner_col * cap + rank_col.astype(jnp.int32)
    pos_row = pos_col.astype(F32).T.astype(jnp.int32)
    pick_f = jnp.where((pos_row == sub) & live_row, 1.0, 0.0)
    pick_tf = jnp.where((pos_col == lane) & live_col, 1.0, 0.0)
    local = ids_row - owner_row * blocks_dev
    local = local // 2 + half * (local - (local // 2) * 2)
    asked = jnp.sum(pick_f * (local + 1).astype(F32), axis=1, keepdims=True) - 1.0
    asks_mine[...] = jnp.broadcast_to(asked, square).reshape(owners, cap, LANES)
    pick[:, :pairs] = pick_f[:, :pairs].astype(BF16)
    pick[:, pairs:] = pick_f[:, :pairs].astype(BF16)
    pick_t[...] = pick_tf[:pairs, :].astype(BF16)
    hot_slab = jnp.where((slab_row == sub.astype(F32)) & live_row, 1.0, 0.0)
    hot_slab_t = hot_slab.T
    sums_by_slab[:, :pairs] = hot_slab[:slabs, :pairs].astype(BF16)
    sums_by_slab[:, pairs:] = hot_slab[:slabs, :pairs].astype(BF16)
    slab_hot_t[:, :slabs] = hot_slab_t[:pairs, :slabs].astype(BF16)
    slab_hot_t[:, slabs:] = hot_slab_t[:pairs, :slabs].astype(BF16)

    wide = (half, LANES)
    low_lane = iota(wide, 1) < BLOCK

    def to_rows(source, target):
        for r in range(half):
            cols = pl.ds(r * LANES, LANES)
            flat[pl.ds(r, 8, stride=half), :] = source[0:8, cols]
            flat[8 * half + r : 8 * half + r + 1, :] = source[8:9, cols]
        for i in range(5):
            left = flat[pl.ds(2 * i * half, half), :]
            if i < 4:
                right = flat[pl.ds((2 * i + 1) * half, half), :]
            else:
                right = jnp.zeros(wide, F32)
            cols = pl.ds(i * LANES, LANES)
            target[0:half, cols] = jnp.where(low_lane, left, pltpu.roll(right, BLOCK, 1))
            target[half:, cols] = jnp.where(low_lane, pltpu.roll(left, BLOCK, 1), right)

    def from_rows(value, target):
        for i in range(5):
            even = value[0:half, i * LANES : (i + 1) * LANES]
            odd = value[half:, i * LANES : (i + 1) * LANES]
            target[2 * i] = jnp.where(low_lane, even, pltpu.roll(odd, BLOCK, 1))
            if i < 4:
                target[2 * i + 1] = jnp.where(low_lane, pltpu.roll(even, BLOCK, 1), odd)

    to_rows(rs_ref, v0)
    to_rows(damp_ref, damp)

    pl.semaphore_wait(barrier, owners + ncam - 2)

    def pt_exchange(sources, target, send_sem, recv_sem):
        copies = []
        for hop in range(1, owners):
            peer = lax.rem(me_pt + hop, owners)
            copy = pltpu.make_async_remote_copy(
                src_ref=sources(peer), dst_ref=target,
                send_sem=send_sem.at[hop - 1], recv_sem=recv_sem.at[hop - 1],
                device_id=at_pt(peer), device_id_type=MESH,
            )
            copy.start()
            copies.append(copy)
        return copies

    def wait_all(copies):
        for copy in copies:
            copy.wait()

    ask_copies = pt_exchange(lambda peer: asks_mine.at[peer], asks.at[me_pt], ask_send, ask_recv)
    asks[me_pt] = asks_mine[me_pt]

    def to_sibling(source, target, sems, c):
        copy = pltpu.make_async_remote_copy(
            src_ref=source, dst_ref=target, send_sem=sems.at[0, c], recv_sem=sems.at[1, c],
            device_id=at_cam(sibling), device_id_type=MESH,
        )
        copy.start()
        return [copy]

    def to_far(source, target, sems, c):
        copies = []
        for hop in range(1, nx):
            peer = far(hop)
            copy = pltpu.make_async_remote_copy(
                src_ref=source(peer), dst_ref=target(hop),
                send_sem=sems.at[0, c, hop - 1], recv_sem=sems.at[1, c, hop - 1],
                device_id=at_cam(peer * 2 + me_core), device_id_type=MESH,
            )
            copy.start()
            copies.append(copy)
        return copies

    def put_parts(buf, c, k, value):
        for q in range(ncam):
            buf[c, q % 2, q // 2, k] = value[:, q * part : (q + 1) * part]

    short_low = iota((cap // 2, LANES), 1) < BLOCK

    def pack(value, buf, first, last):
        for o in range(owners):
            rows = value[o * cap : (o + 1) * cap]
            for i in range(first, last):
                part_of = rows[:, (i - first) * LANES : (i - first + 1) * LANES]
                if i < 4:
                    buf[o, i * cap : (i + 1) * cap, :] = part_of
                else:
                    buf[o, 4 * cap :, :] = jnp.where(
                        short_low, part_of[: cap // 2], pltpu.roll(part_of[cap // 2 :], BLOCK, 1)
                    )

    def unpack(buf):
        tall = []
        for o in range(owners):
            cols = [buf[o, i * cap : (i + 1) * cap, :] for i in range(4)]
            last = buf[o, 4 * cap :, :]
            zero = jnp.zeros_like(last)
            last = [
                jnp.where(short_low, last, zero),
                jnp.where(short_low, pltpu.roll(last, BLOCK, 1), zero),
            ]
            cols.append(jnp.concatenate(last, axis=0))
            tall.append(jnp.concatenate(cols, axis=1))
        return jnp.concatenate(tall, axis=0)

    def send_blocks(vec, it):
        pack(select_rows(place[...], vec[...]), packed.at[it], 0, 5)
        got[it, me_pt] = packed[it, me_pt]
        return pt_exchange(
            lambda peer: packed.at[it, peer], got.at[it, me_pt], a_send.at[it], a_recv.at[it]
        )

    def make_tables(it):
        value = select_rows(pick_t[...], unpack(got.at[it]))
        for i in range(5):
            here = value[:, i * LANES : (i + 1) * LANES]
            tables[2 * i] = here
            if i < 4:
                tables[2 * i + 1] = pltpu.roll(here, BLOCK, 1)

    h_copies = []
    for c in range(CHUNKS):
        jp_loads[c].wait()
        if c == CHUNKS // 2:
            wait_all(ask_copies)
            wanted = asks[...].reshape(spots, LANES)
            hot = jnp.where(wanted == lane.astype(F32), 1.0, 0.0)
            place[...] = hot[:, : 2 * half].astype(BF16)
            place_t[...] = hot.T[: 2 * half, :].astype(BF16)
            a_copies = send_blocks(v0, 0)

        def hess_tile(t, carry, c=c):
            col = pl.multiple_of(c * width + t * LANES, LANES)
            spot = pl.ds(pl.multiple_of(t * LANES, LANES), LANES)
            for g in range(pairs // 16):
                rows = slice(g * 16, g * 16 + 16)
                point = [jp[k, rows, pl.ds(col, LANES)].astype(F32) for k in range(6)]
                for f, (a, b) in enumerate(HESS):
                    high, low = split2(point[a] * point[b] + point[3 + a] * point[3 + b])
                    tbuf[f, rows, spot] = high
                    tbuf[f, pairs + g * 16 : pairs + g * 16 + 16, spot] = low
            return carry

        lax.fori_loop(0, width // LANES, hess_tile, 0)
        for f in range(6):
            put_parts(h_part, c, f, dot(sums_by_slab[...], tbuf[f]))
        h_copies.append(to_sibling(h_part.at[c, 1 - me_core], h_sib.at[c], hs_sem, c))

    h_far_copies = []
    for c in range(CHUNKS):
        wait_all(h_copies[c])
        h_red[c] = h_part[c, me_core] + h_sib[c]
        h_far_copies.append(
            to_far(lambda peer: h_red.at[c, peer], lambda hop: h_far.at[c, hop - 1], hx_sem, c)
        )

    idx_load.wait()

    def hot_tile(t, carry):
        cols = pl.ds(pl.multiple_of(t * LANES, LANES), LANES)
        cams = iota((BLOCK // 2, LANES), 0)
        here = idx[:, cols] & (BLOCK // 2 - 1)
        for j in range(pairs):
            line = jnp.broadcast_to(here[j : j + 1, :], (BLOCK // 2, LANES))
            hots[j * BLOCK // 2 : (j + 1) * BLOCK // 2, cols] = jnp.where(
                cams == line, 1.0, 0.0
            ).astype(BF16)
        return carry

    lax.fori_loop(0, points // LANES, hot_tile, 0)

    def finish_hessian(c):
        wait_all(h_far_copies[c])
        for t in range(part // LANES):
            cols = pl.ds(t * LANES, LANES)
            hess = []
            for f in range(6):
                total = h_red[c, me_x, f, :, cols]
                for hop in range(1, nx):
                    total = total + h_far[c, hop - 1, f, :, cols]
                hess.append(total)
            tile = (c * width + me_cam * part) // LANES + t
            damping = pdamp_ref[pl.ds(tile, slabs, stride=row_tiles), :]
            for f, value in enumerate(invert(hess, damping)):
                inverse[c, f, :, cols] = value

    def forward(c, it):
        if it == 0:
            jc_loads[c].wait()

        def tile(t, carry):
            col = pl.multiple_of(c * width + t * LANES, LANES)
            cols = pl.ds(col, LANES)
            spot = pl.ds(pl.multiple_of(t * LANES, LANES), LANES)
            for g in range(pairs // 16):
                rows = slice(g * 16, g * 16 + 16)
                index = idx[rows, cols]
                pr = [None, None]
                for k in range(9):
                    at_camera = jnp.take_along_axis(
                        tables[k, rows, :], index, axis=1, mode="promise_in_bounds"
                    )
                    for i in range(2):
                        term = jc[9 * i + k, rows, cols].astype(F32) * at_camera
                        pr[i] = term if k == 0 else pr[i] + term
                for i in range(2):
                    proj[i, rows, cols] = pr[i]
                for f in range(3):
                    made = (
                        jp[f, rows, cols].astype(F32) * pr[0]
                        + jp[3 + f, rows, cols].astype(F32) * pr[1]
                    )
                    high, low = split2(made)
                    tbuf[f, rows, spot] = high
                    tbuf[f, pairs + g * 16 : pairs + g * 16 + 16, spot] = low
            return carry

        lax.fori_loop(0, width // LANES, tile, 0)
        for f in range(3):
            put_parts(y_part.at[it], c, f, dot(sums_by_slab[...], tbuf[f]))
        return to_sibling(
            y_part.at[it, c, 1 - me_core], y_sib.at[it, c], ys_sem.at[it], c
        )

    def reduce_sibling(c, it, copies):
        wait_all(copies)
        y_red[it, c] = y_part[it, c, me_core] + y_sib[it, c]
        return to_far(
            lambda peer: y_red.at[it, c, peer],
            lambda hop: y_far.at[it, c, hop - 1],
            yx_sem.at[it], c,
        )

    def eliminate(c, it, copies):
        if it == 0:
            finish_hessian(c)
        wait_all(copies)
        vec = []
        for f in range(3):
            total = y_red[it, c, me_x, f]
            for hop in range(1, nx):
                total = total + y_far[it, c, hop - 1, f]
            vec.append(total)
        for f, value in enumerate(apply_inverse([inverse[c, f] for f in range(6)], vec)):
            z_all[it, c, me_core, me_x, f] = value
        here = z_all.at[it, c, me_core, me_x]
        return to_far(lambda peer: here, lambda hop: here, zx_sem.at[it], c)

    def share(c, it, copies):
        wait_all(copies)
        here = z_all.at[it, c, me_core]
        return to_sibling(here, here, zs_sem.at[it], c)

    def backward(c, it, copies):
        wait_all(copies)
        for q in range(ncam):
            for f in range(3):
                high, low = split2(z_all[it, c, q % 2, q // 2, f])
                zslot[f, :, q * part : (q + 1) * part] = dot(
                    slab_hot_t[...], jnp.concatenate([high, low], axis=0)
                )

        def build(g):
            base = pl.multiple_of(g * 16, 16)
            rows = pl.ds(base, 16)
            for t in range(width // LANES):
                cols = pl.ds(c * width + t * LANES, LANES)
                spot = pl.ds(t * LANES, LANES)
                miss = [proj[i, rows, cols] for i in range(2)]
                for f in range(3):
                    z = zslot[f, rows, spot]
                    for i in range(2):
                        miss[i] = miss[i] - jp[3 * i + f, rows, cols].astype(F32) * z
                push = [
                    jc[k, rows, cols].astype(F32) * miss[0]
                    + jc[9 + k, rows, cols].astype(F32) * miss[1]
                    for k in range(9)
                ]
                upper = jnp.where(idx[rows, cols] >= BLOCK // 2, 1.0, 0.0)
                for h in range(2):
                    mine = [value[h * 8 : h * 8 + 8] for value in push]
                    last_high = mine[8].astype(BF16).astype(F32)
                    halves = upper[h * 8 : h * 8 + 8]
                    halves = jnp.concatenate([halves, halves], axis=0).astype(BF16) > 0.5
                    tiles = [None] * 9
                    for i in range(4):
                        pair = jnp.concatenate([mine[2 * i], mine[2 * i + 1]], axis=0)
                        tiles[i], tiles[5 + i] = split2(pair)
                    pair = jnp.concatenate([last_high, mine[8] - last_high], axis=0)
                    tiles[4] = pair.astype(BF16)
                    for i, value in enumerate(tiles):
                        pbuf[h, 16 * i : 16 * i + 16, spot] = value
                        above = jnp.where(halves, value, jnp.zeros_like(value))
                        pbuf[h, 144 + 16 * i : 160 + 16 * i, spot] = above

        def scatter(g):
            base = g * 16
            for h in range(2):
                total = None
                for t in range(width // KCOLS):
                    cols = pl.ds(c * width + t * KCOLS, KCOLS)
                    hot_rows = pl.ds(pl.multiple_of((base + h * 8) * (BLOCK // 2), 256), 4 * BLOCK)
                    piece = lax.dot_general(
                        pbuf[h, :, t * KCOLS : (t + 1) * KCOLS],
                        hots[hot_rows, cols],
                        (((1,), (1,)), ((), ())),
                        preferred_element_type=F32,
                    )
                    total = piece if total is None else total + piece
                if c == 0:
                    acc[2 * g + h] = total
                else:
                    acc[2 * g + h] += total

        groups = pairs // 16

        def group(g, carry):
            build(g)
            scatter(g)
            return carry

        lax.fori_loop(0, groups, group, 0)

    def slot_sums(first, last):
        small = (8, LANES)
        row = iota(small, 0)
        quarter = iota(small, 1) // (BLOCK // 2)
        first4 = row < 4
        turn = lax.rem(row, 4)

        def one(g, carry):
            rows = pl.ds(pl.multiple_of(g * 8, 8), 8)
            for i in range(first, last):
                line = jnp.zeros(small, F32)
                for q in range(4 if i < 4 else 2):
                    f = 2 * i + q // 2
                    if q % 2 == 0:
                        parts = []
                        for top in (0, 144):
                            low = top + (72 if f == 8 else 80 + 8 * f)
                            parts.append(
                                acc[g, top + 8 * f : top + 8 * f + 8, :] + acc[g, low : low + 8, :]
                            )
                    both = parts[0] - parts[1] if q % 2 == 0 else parts[1]
                    here = jnp.where(first4, both[:, :LANES], both[:, LANES:])
                    moved = None
                    for k in range(4):
                        shift = (32 * (q - k)) % LANES
                        turned = pltpu.roll(here, shift, 1) if shift else here
                        moved = turned if k == 0 else jnp.where(turn == k, turned, moved)
                    line = jnp.where(quarter == q, moved, line)
                slotsum[rows, i * LANES : (i + 1) * LANES] = line
            return carry

        lax.fori_loop(0, pairs // 8, one, 0)

    def schur(vec, it, a_copies, beside):
        wait_all(a_copies)
        make_tables(it)
        next(beside, None)
        first, second, third, fourth = {}, {}, {}, {}
        for step in range(CHUNKS + 4):
            if step < CHUNKS:
                first[step] = forward(step, it)
                next(beside, None)
            if 0 <= step - 1 < CHUNKS:
                second[step - 1] = reduce_sibling(step - 1, it, first[step - 1])
            if 0 <= step - 2 < CHUNKS:
                third[step - 2] = eliminate(step - 2, it, second[step - 2])
            if 0 <= step - 3 < CHUNKS:
                fourth[step - 3] = share(step - 3, it, third[step - 3])
            if step - 4 >= 0:
                backward(step - 4, it, fourth[step - 4])
        copies = []
        for n, (first, last) in enumerate(((0, 2), (2, 5))):
            slot_sums(first, last)
            high, low = split2(slotsum[:, first * LANES : last * LANES])
            rows = slice(first * cap, last * cap if n == 0 else 4 * cap + cap // 2)
            pack(
                dot(pick[...], jnp.concatenate([high, low], axis=0)), out_pack.at[it], first, last
            )
            copies += pt_exchange(
                lambda peer: out_pack.at[it, peer, rows], in_pack.at[it, me_pt, rows],
                e_send.at[it, n], e_recv.at[it, n],
            )
        in_pack[it, me_pt] = out_pack[it, me_pt]
        next(beside, None)
        wait_all(copies)
        high, low = split2(unpack(in_pack.at[it]))
        total = dot(place_t[...], high) + dot(place_t[...], low)
        return damp[...] * vec[...] + total

    def fill(value):
        return jnp.broadcast_to(jnp.sum(value, keepdims=True), (8, LANES))

    def start_dots(values, n):
        for k, value in enumerate(values):
            dots[n, k] = fill(value)
        copies = []
        for hop in range(1, owners):
            copy = pltpu.make_async_remote_copy(
                src_ref=dots.at[n], dst_ref=dots_pt.at[n, hop - 1],
                send_sem=dp_sem.at[0, n, hop - 1], recv_sem=dp_sem.at[1, n, hop - 1],
                device_id=at_pt(lax.rem(me_pt + hop, owners)), device_id_type=MESH,
            )
            copy.start()
            copies.append(copy)
        return copies

    def pass_dots(copies, n):
        wait_all(copies)
        total = dots[n]
        for hop in range(1, owners):
            total = total + dots_pt[n, hop - 1]
        dots_cam[n, 0] = total
        copies = []
        for hop in range(1, ncam):
            copy = pltpu.make_async_remote_copy(
                src_ref=dots_cam.at[n, 0], dst_ref=dots_cam.at[n, hop],
                send_sem=dc_sem.at[0, n, hop - 1], recv_sem=dc_sem.at[1, n, hop - 1],
                device_id=at_cam(lax.rem(me_cam + hop, ncam)), device_id_type=MESH,
            )
            copy.start()
            copies.append(copy)
        return copies

    def end_dots(copies, n, k):
        wait_all(copies)
        total = dots_cam[n, 0]
        for hop in range(1, ncam):
            total = total + dots_cam[n, hop]
        return [total[i][0:1, 0:1] for i in range(k)]

    v1[...] = schur(v0, 0, a_copies, iter(()))
    a_copies = send_blocks(v1, 1)
    known = []

    def scalars(copies):
        copies = pass_dots(copies, 0)
        yield
        yield
        norm0, curve0 = end_dots(copies, 0, 2)
        step0 = norm0 / curve0
        res1 = v0[...] - step0 * v1[...]
        copies = start_dots([res1 * res1], 1)
        yield
        yield
        copies = pass_dots(copies, 1)
        yield
        (norm1,) = end_dots(copies, 1, 1)
        known.extend([norm0, norm1, step0])
        yield

    copies = start_dots([v0[...] * v0[...], v0[...] * v1[...]], 0)
    v2[...] = schur(v1, 1, a_copies, scalars(copies))
    norm0, norm1, step0 = known
    res1 = v0[...] - step0 * v1[...]
    ratio = norm1 / norm0
    dir1 = res1 + ratio * v0[...]
    image1 = v1[...] - step0 * v2[...] + ratio * v1[...]
    three = start_dots([dir1 * image1], 2)
    three = pass_dots(three, 2)
    (curve1,) = end_dots(three, 2, 1)
    step1 = norm1 / curve1
    from_rows(step0 * v0[...] + step1 * dir1, answer_ref)
    from_rows(res1 - step1 * image1, residual_ref)


def per_device(
    right_side, cam_damping, point_damping, block_ids, slab_ids, cam_index, cam_jacobian,
    point_jacobian, pair_count,
):
    pairs = block_ids.shape[2]
    points = cam_index.shape[3]
    slabs = point_damping.shape[0] // points
    cam_dev = right_side.shape[1]
    blocks_dev = cam_dev // BLOCK
    owners = lax.axis_size("pt")
    ncam = lax.axis_size("cam")
    nx = ncam // 2
    spots = 2 * pairs
    cap = spots // owners
    width = points // CHUNKS
    part = width // ncam
    idx = cam_index.reshape(pairs, points)
    jc = cam_jacobian.reshape(pairs, 18, points).transpose(1, 0, 2)
    jp = point_jacobian.reshape(pairs, 6, points).transpose(1, 0, 2)
    vmem = pl.BlockSpec(memory_space=pltpu.VMEM)
    hbm = pl.BlockSpec(memory_space=pl.ANY)
    V = pltpu.VMEM
    D = pltpu.SemaphoreType.DMA
    far = max(nx - 1, 1)
    scratch = [
        V((pairs, points), jnp.int32), V((18, pairs, points), BF16), V((6, pairs, points), BF16),
        V((pairs * BLOCK // 2, points), BF16),
        D((2 * CHUNKS + 1,)),
        V((spots, blocks_dev), BF16), V((blocks_dev, spots), BF16),
        V((spots, 2 * pairs), BF16), V((pairs, spots), BF16),
        V((slabs, 2 * pairs), BF16), V((pairs, 2 * slabs), BF16),
        V((owners, cap, LANES), F32), V((owners, cap, LANES), F32),
        V((9 * blocks_dev // 2, LANES), F32),
        V((blocks_dev, COLS), F32), V((blocks_dev, COLS), F32), V((blocks_dev, COLS), F32),
        V((blocks_dev, COLS), F32),
        V((ITERS, owners, 4 * cap + cap // 2, LANES), F32),
        V((ITERS, owners, 4 * cap + cap // 2, LANES), F32),
        V((9, pairs, LANES), F32),
        V((2, pairs, points), F32),
        V((6, 2 * pairs, width), BF16),
        V((3, pairs, width), F32),
        V((2, 288, width), BF16),
        V((pairs // 8, 288, 4 * BLOCK), F32),
        V((pairs, COLS), F32),
        V((CHUNKS, 2, nx, 6, slabs, part), F32), V((CHUNKS, nx, 6, slabs, part), F32),
        V((CHUNKS, nx, 6, slabs, part), F32), V((CHUNKS, far, 6, slabs, part), F32),
        V((CHUNKS, 6, slabs, part), F32),
        V((ITERS, CHUNKS, 2, nx, 3, slabs, part), F32), V((ITERS, CHUNKS, nx, 3, slabs, part), F32),
        V((ITERS, CHUNKS, nx, 3, slabs, part), F32), V((ITERS, CHUNKS, far, 3, slabs, part), F32),
        V((ITERS, CHUNKS, 2, nx, 3, slabs, part), F32),
        V((ITERS, owners, 4 * cap + cap // 2, LANES), F32),
        V((ITERS, owners, 4 * cap + cap // 2, LANES), F32),
        V((3, 2, 8, LANES), F32), V((3, owners - 1, 2, 8, LANES), F32),
        V((3, ncam, 2, 8, LANES), F32),
        D((owners - 1,)), D((owners - 1,)),
        D((ITERS, owners - 1)), D((ITERS, owners - 1)),
        D((ITERS, 2, owners - 1)), D((ITERS, 2, owners - 1)),
        D((2, CHUNKS)), D((2, CHUNKS, far)),
        D((ITERS, 2, CHUNKS)), D((ITERS, 2, CHUNKS, far)),
        D((ITERS, 2, CHUNKS, far)), D((ITERS, 2, CHUNKS)),
        D((2, 3, owners - 1)), D((2, 3, ncam - 1)),
    ]
    outs = pl.pallas_call(
        body,
        name="cg",
        out_shape=[jax.ShapeDtypeStruct((9, blocks_dev // 2, LANES), F32)] * 2,
        in_specs=[vmem] * 6 + [hbm] * 3,
        out_specs=[vmem] * 2,
        scratch_shapes=scratch,
        compiler_params=pltpu.CompilerParams(
            collective_id=0, has_side_effects=True, vmem_limit_bytes=VMEM_BYTES
        ),
    )(
        block_ids.reshape(1, pairs), slab_ids.reshape(1, pairs), pair_count.reshape(1, 1),
        right_side, cam_damping, point_damping.reshape(-1, LANES), idx, jc, jp,
    )
    return outs[0].reshape(9, cam_dev), outs[1].reshape(9, cam_dev)


def solution(mesh):
    in_specs = (
        P(None, ("cam", "pt")),
        P(None, ("cam", "pt")),
        P("pt"),
        P("cam", "pt", None),
        P("cam", "pt", None),
        P("cam", "pt", None, None),
        P("cam", "pt", None, None, None),
        P("cam", "pt", None, None, None),
        P("cam", "pt"),
    )
    out_specs = (P(None, ("cam", "pt")), P(None, ("cam", "pt")))
    return jax.shard_map(
        per_device, mesh=mesh, in_specs=in_specs, out_specs=out_specs, check_vma=False
    )
```

```python
import functools

import jax
import jax.numpy as jnp
from jax import lax
from jax.experimental import pallas as pl
from jax.experimental.pallas import tpu as pltpu
from jax.sharding import PartitionSpec as P

BLOCK = 64
ITERS = 2
LANES = 128
CHUNKS = 4
COLS = 5 * LANES
KCOLS = 4 * LANES
F32 = jnp.float32
BF16 = jnp.bfloat16
VMEM_BYTES = 60 * 1024 * 1024
MESH = pl.DeviceIdType.MESH
HESS = [(0, 0), (1, 1), (2, 2), (0, 1), (1, 2), (0, 2)]


def iota(shape, axis):
    return lax.broadcasted_iota(jnp.int32, shape, axis)


def split2(value):
    high = value.astype(BF16)
    return high, (value - high.astype(F32)).astype(BF16)


def split3(value):
    high, low = split2(value)
    last = value - high.astype(F32) - low.astype(F32)
    return high, low, last.astype(BF16)


def dot(a, b):
    return jnp.dot(a, b, preferred_element_type=F32)


def select_rows(hot, value):
    parts = split3(value)
    return dot(hot, parts[0]) + dot(hot, parts[1]) + dot(hot, parts[2])


def invert(hess, damping):
    xx, yy, zz = (hess[k] + damping for k in range(3))
    xy, yz, xz = hess[3], hess[4], hess[5]
    cof_xx = yy * zz - yz * yz
    cof_xy = xz * yz - xy * zz
    cof_xz = xy * yz - xz * yy
    cof_yy = xx * zz - xz * xz
    cof_yz = xy * xz - xx * yz
    cof_zz = xx * yy - xy * xy
    det = xx * cof_xx + xy * cof_xy + xz * cof_xz
    return [c / det for c in (cof_xx, cof_xy, cof_xz, cof_yy, cof_yz, cof_zz)]


def apply_inverse(inv, vec):
    return [
        inv[0] * vec[0] + inv[1] * vec[1] + inv[2] * vec[2],
        inv[1] * vec[0] + inv[3] * vec[1] + inv[4] * vec[2],
        inv[2] * vec[0] + inv[4] * vec[1] + inv[5] * vec[2],
    ]


def body(
    ids_ref, slab_ref, count_ref, rs_ref, damp_ref, pdamp_ref, idx_hbm, jc_hbm, jp_hbm,
    answer_ref, residual_ref,
    idx, jc, jp, hots, load_sem,
    place, place_t, pick, pick_t, sums_by_slab, slab_hot_t, asks_mine, asks,
    flat, v0, v1, v2, damp, packed, got, tables, proj, tbuf, zslot, pbuf, acc, slotsum,
    h_part, h_sib, h_red, h_far, inverse, y_part, y_sib, y_red, y_far, z_all,
    out_pack, in_pack, dots, dots_pt, dots_cam,
    ask_send, ask_recv, a_send, a_recv, e_send, e_recv,
    hs_sem, hx_sem, ys_sem, yx_sem, zx_sem, zs_sem, dp_sem, dc_sem,
):
    pairs, points = idx.shape
    owners = lax.axis_size("pt")
    ncam = lax.axis_size("cam")
    nx = ncam // 2
    me_pt = lax.axis_index("pt")
    me_cam = lax.axis_index("cam")
    me_x = me_cam // 2
    me_core = lax.rem(me_cam, 2)
    sibling = me_x * 2 + (1 - me_core)
    spots = 2 * pairs
    cap = spots // owners
    slabs = sums_by_slab.shape[0]
    width = points // CHUNKS
    part = width // ncam
    half = v0.shape[0] // 2
    row_tiles = points // LANES

    def far(hop):
        return lax.rem(me_x + hop, nx)

    def at_cam(cam):
        return {"cam": cam}

    def at_pt(pt):
        return {"pt": pt}

    def load(source, target, sem, c):
        cols = pl.ds(c * width, width)
        copy = pltpu.make_async_copy(source.at[:, :, cols], target.at[:, :, cols], sem)
        copy.start()
        return copy

    jp_loads = [load(jp_hbm, jp, load_sem.at[c], c) for c in range(CHUNKS)]
    idx_load = pltpu.make_async_copy(idx_hbm, idx, load_sem.at[2 * CHUNKS])
    idx_load.start()
    jc_loads = [load(jc_hbm, jc, load_sem.at[CHUNKS + c], c) for c in range(CHUNKS)]

    barrier = pltpu.get_barrier_semaphore()
    for hop in range(1, owners):
        pl.semaphore_signal(
            barrier, inc=1, device_id=at_pt(lax.rem(me_pt + hop, owners)), device_id_type=MESH
        )
    for hop in range(1, ncam):
        pl.semaphore_signal(
            barrier, inc=1, device_id=at_cam(lax.rem(me_cam + hop, ncam)), device_id_type=MESH
        )

    square = (LANES, LANES)
    sub, lane = iota(square, 0), iota(square, 1)
    blank = jnp.zeros((1, LANES - pairs), F32)
    ids_row = jnp.concatenate([ids_ref[...].astype(F32), blank], axis=1)
    slab_row = jnp.concatenate([slab_ref[...].astype(F32), blank], axis=1)
    count = jnp.broadcast_to(count_ref[...], square)
    live_row = lane < count
    live_col = sub < count
    ids_row = jnp.broadcast_to(ids_row, square).astype(jnp.int32)
    slab_row = jnp.broadcast_to(slab_row, square)
    ids_col = ids_row.astype(F32).T.astype(jnp.int32)
    blocks_dev = 2 * half
    owner_row = ids_row // blocks_dev
    owner_col = ids_col // blocks_dev
    same = jnp.where(owner_row == owner_col, 1.0, 0.0)
    before = jnp.where((lane < sub) & live_row, same, 0.0)
    rank_col = jnp.broadcast_to(jnp.sum(before, axis=1, keepdims=True), square)
    pos_col = owner_col * cap + rank_col.astype(jnp.int32)
    pos_row = pos_col.astype(F32).T.astype(jnp.int32)
    pick_f = jnp.where((pos_row == sub) & live_row, 1.0, 0.0)
    pick_tf = jnp.where((pos_col == lane) & live_col, 1.0, 0.0)
    local = ids_row - owner_row * blocks_dev
    local = local // 2 + half * (local - (local // 2) * 2)
    asked = jnp.sum(pick_f * (local + 1).astype(F32), axis=1, keepdims=True) - 1.0
    asks_mine[...] = jnp.broadcast_to(asked, square).reshape(owners, cap, LANES)
    pick[:, :pairs] = pick_f[:, :pairs].astype(BF16)
    pick[:, pairs:] = pick_f[:, :pairs].astype(BF16)
    pick_t[...] = pick_tf[:pairs, :].astype(BF16)
    hot_slab = jnp.where((slab_row == sub.astype(F32)) & live_row, 1.0, 0.0)
    hot_slab_t = hot_slab.T
    sums_by_slab[:, :pairs] = hot_slab[:slabs, :pairs].astype(BF16)
    sums_by_slab[:, pairs:] = hot_slab[:slabs, :pairs].astype(BF16)
    slab_hot_t[:, :slabs] = hot_slab_t[:pairs, :slabs].astype(BF16)
    slab_hot_t[:, slabs:] = hot_slab_t[:pairs, :slabs].astype(BF16)

    wide = (half, LANES)
    low_lane = iota(wide, 1) < BLOCK

    def to_rows(source, target):
        for r in range(half):
            cols = pl.ds(r * LANES, LANES)
            flat[pl.ds(r, 8, stride=half), :] = source[0:8, cols]
            flat[8 * half + r : 8 * half + r + 1, :] = source[8:9, cols]
        for i in range(5):
            left = flat[pl.ds(2 * i * half, half), :]
            if i < 4:
                right = flat[pl.ds((2 * i + 1) * half, half), :]
            else:
                right = jnp.zeros(wide, F32)
            cols = pl.ds(i * LANES, LANES)
            target[0:half, cols] = jnp.where(low_lane, left, pltpu.roll(right, BLOCK, 1))
            target[half:, cols] = jnp.where(low_lane, pltpu.roll(left, BLOCK, 1), right)

    def from_rows(value, target):
        for i in range(5):
            even = value[0:half, i * LANES : (i + 1) * LANES]
            odd = value[half:, i * LANES : (i + 1) * LANES]
            target[2 * i] = jnp.where(low_lane, even, pltpu.roll(odd, BLOCK, 1))
            if i < 4:
                target[2 * i + 1] = jnp.where(low_lane, pltpu.roll(even, BLOCK, 1), odd)

    to_rows(rs_ref, v0)
    to_rows(damp_ref, damp)

    pl.semaphore_wait(barrier, owners + ncam - 2)

    def pt_exchange(sources, target, send_sem, recv_sem):
        copies = []
        for hop in range(1, owners):
            peer = lax.rem(me_pt + hop, owners)
            copy = pltpu.make_async_remote_copy(
                src_ref=sources(peer), dst_ref=target,
                send_sem=send_sem.at[hop - 1], recv_sem=recv_sem.at[hop - 1],
                device_id=at_pt(peer), device_id_type=MESH,
            )
            copy.start()
            copies.append(copy)
        return copies

    def wait_all(copies):
        for copy in copies:
            copy.wait()

    ask_copies = pt_exchange(lambda peer: asks_mine.at[peer], asks.at[me_pt], ask_send, ask_recv)
    asks[me_pt] = asks_mine[me_pt]

    def to_sibling(source, target, sems, c):
        copy = pltpu.make_async_remote_copy(
            src_ref=source, dst_ref=target, send_sem=sems.at[0, c], recv_sem=sems.at[1, c],
            device_id=at_cam(sibling), device_id_type=MESH,
        )
        copy.start()
        return [copy]

    def to_far(source, target, sems, c):
        copies = []
        for hop in range(1, nx):
            peer = far(hop)
            copy = pltpu.make_async_remote_copy(
                src_ref=source(peer), dst_ref=target(hop),
                send_sem=sems.at[0, c, hop - 1], recv_sem=sems.at[1, c, hop - 1],
                device_id=at_cam(peer * 2 + me_core), device_id_type=MESH,
            )
            copy.start()
            copies.append(copy)
        return copies

    def put_parts(buf, c, k, value):
        for q in range(ncam):
            buf[c, q % 2, q // 2, k] = value[:, q * part : (q + 1) * part]

    short_low = iota((cap // 2, LANES), 1) < BLOCK

    def pack(value, buf, first, last):
        for o in range(owners):
            rows = value[o * cap : (o + 1) * cap]
            for i in range(first, last):
                part_of = rows[:, (i - first) * LANES : (i - first + 1) * LANES]
                if i < 4:
                    buf[o, i * cap : (i + 1) * cap, :] = part_of
                else:
                    buf[o, 4 * cap :, :] = jnp.where(
                        short_low, part_of[: cap // 2], pltpu.roll(part_of[cap // 2 :], BLOCK, 1)
                    )

    def unpack(buf):
        tall = []
        for o in range(owners):
            cols = [buf[o, i * cap : (i + 1) * cap, :] for i in range(4)]
            last = buf[o, 4 * cap :, :]
            zero = jnp.zeros_like(last)
            last = [
                jnp.where(short_low, last, zero),
                jnp.where(short_low, pltpu.roll(last, BLOCK, 1), zero),
            ]
            cols.append(jnp.concatenate(last, axis=0))
            tall.append(jnp.concatenate(cols, axis=1))
        return jnp.concatenate(tall, axis=0)

    def send_blocks(vec, it):
        pack(select_rows(place[...], vec[...]), packed.at[it], 0, 5)
        got[it, me_pt] = packed[it, me_pt]
        return pt_exchange(
            lambda peer: packed.at[it, peer], got.at[it, me_pt], a_send.at[it], a_recv.at[it]
        )

    def make_tables(it):
        value = select_rows(pick_t[...], unpack(got.at[it]))
        for i in range(5):
            here = value[:, i * LANES : (i + 1) * LANES]
            tables[2 * i] = here
            if i < 4:
                tables[2 * i + 1] = pltpu.roll(here, BLOCK, 1)

    h_copies = []
    for c in range(CHUNKS):
        jp_loads[c].wait()
        if c == CHUNKS // 2:
            wait_all(ask_copies)
            wanted = asks[...].reshape(spots, LANES)
            hot = jnp.where(wanted == lane.astype(F32), 1.0, 0.0)
            place[...] = hot[:, : 2 * half].astype(BF16)
            place_t[...] = hot.T[: 2 * half, :].astype(BF16)
            a_copies = send_blocks(v0, 0)

        def hess_tile(t, carry, c=c):
            col = pl.multiple_of(c * width + t * LANES, LANES)
            spot = pl.ds(pl.multiple_of(t * LANES, LANES), LANES)
            for g in range(pairs // 16):
                rows = slice(g * 16, g * 16 + 16)
                point = [jp[k, rows, pl.ds(col, LANES)].astype(F32) for k in range(6)]
                for f, (a, b) in enumerate(HESS):
                    high, low = split2(point[a] * point[b] + point[3 + a] * point[3 + b])
                    tbuf[f, rows, spot] = high
                    tbuf[f, pairs + g * 16 : pairs + g * 16 + 16, spot] = low
            return carry

        lax.fori_loop(0, width // LANES, hess_tile, 0, unroll=2)
        for f in range(6):
            put_parts(h_part, c, f, dot(sums_by_slab[...], tbuf[f]))
        h_copies.append(to_sibling(h_part.at[c, 1 - me_core], h_sib.at[c], hs_sem, c))

    h_far_copies = []
    for c in range(CHUNKS):
        wait_all(h_copies[c])
        h_red[c] = h_part[c, me_core] + h_sib[c]
        h_far_copies.append(
            to_far(lambda peer: h_red.at[c, peer], lambda hop: h_far.at[c, hop - 1], hx_sem, c)
        )

    idx_load.wait()

    def hot_tile(t, carry):
        cols = pl.ds(pl.multiple_of(t * LANES, LANES), LANES)
        cams = iota((BLOCK // 2, LANES), 0)
        here = idx[:, cols] & (BLOCK // 2 - 1)
        for j in range(pairs):
            line = jnp.broadcast_to(here[j : j + 1, :], (BLOCK // 2, LANES))
            hots[j * BLOCK // 2 : (j + 1) * BLOCK // 2, cols] = jnp.where(
                cams == line, 1.0, 0.0
            ).astype(BF16)
        return carry

    lax.fori_loop(0, points // LANES, hot_tile, 0)

    def finish_hessian(c):
        wait_all(h_far_copies[c])
        for t in range(part // LANES):
            cols = pl.ds(t * LANES, LANES)
            hess = []
            for f in range(6):
                total = h_red[c, me_x, f, :, cols]
                for hop in range(1, nx):
                    total = total + h_far[c, hop - 1, f, :, cols]
                hess.append(total)
            tile = (c * width + me_cam * part) // LANES + t
            damping = pdamp_ref[pl.ds(tile, slabs, stride=row_tiles), :]
            for f, value in enumerate(invert(hess, damping)):
                inverse[c, f, :, cols] = value

    def forward(c, it):
        if it == 0:
            jc_loads[c].wait()

        def tile(t, carry):
            col = pl.multiple_of(c * width + t * LANES, LANES)
            cols = pl.ds(col, LANES)
            spot = pl.ds(pl.multiple_of(t * LANES, LANES), LANES)
            for g in range(pairs // 16):
                rows = slice(g * 16, g * 16 + 16)
                index = idx[rows, cols]
                pr = [None, None]
                for k in range(9):
                    at_camera = jnp.take_along_axis(
                        tables[k, rows, :], index, axis=1, mode="promise_in_bounds"
                    )
                    for i in range(2):
                        term = jc[9 * i + k, rows, cols].astype(F32) * at_camera
                        pr[i] = term if k == 0 else pr[i] + term
                for i in range(2):
                    proj[i, rows, cols] = pr[i]
                for f in range(3):
                    made = (
                        jp[f, rows, cols].astype(F32) * pr[0]
                        + jp[3 + f, rows, cols].astype(F32) * pr[1]
                    )
                    high, low = split2(made)
                    tbuf[f, rows, spot] = high
                    tbuf[f, pairs + g * 16 : pairs + g * 16 + 16, spot] = low
            return carry

        lax.fori_loop(0, width // LANES, tile, 0, unroll=2)
        for f in range(3):
            put_parts(y_part.at[it], c, f, dot(sums_by_slab[...], tbuf[f]))
        return to_sibling(
            y_part.at[it, c, 1 - me_core], y_sib.at[it, c], ys_sem.at[it], c
        )

    def reduce_sibling(c, it, copies):
        wait_all(copies)
        y_red[it, c] = y_part[it, c, me_core] + y_sib[it, c]
        return to_far(
            lambda peer: y_red.at[it, c, peer],
            lambda hop: y_far.at[it, c, hop - 1],
            yx_sem.at[it], c,
        )

    def eliminate(c, it, copies):
        if it == 0:
            finish_hessian(c)
        wait_all(copies)
        vec = []
        for f in range(3):
            total = y_red[it, c, me_x, f]
            for hop in range(1, nx):
                total = total + y_far[it, c, hop - 1, f]
            vec.append(total)
        for f, value in enumerate(apply_inverse([inverse[c, f] for f in range(6)], vec)):
            z_all[it, c, me_core, me_x, f] = value
        here = z_all.at[it, c, me_core, me_x]
        return to_far(lambda peer: here, lambda hop: here, zx_sem.at[it], c)

    def share(c, it, copies):
        wait_all(copies)
        here = z_all.at[it, c, me_core]
        return to_sibling(here, here, zs_sem.at[it], c)

    def backward(c, it, copies):
        wait_all(copies)
        for q in range(ncam):
            for f in range(3):
                high, low = split2(z_all[it, c, q % 2, q // 2, f])
                zslot[f, :, q * part : (q + 1) * part] = dot(
                    slab_hot_t[...], jnp.concatenate([high, low], axis=0)
                )

        def build(g):
            base = pl.multiple_of(g * 16, 16)
            rows = pl.ds(base, 16)
            for t in range(width // LANES):
                cols = pl.ds(c * width + t * LANES, LANES)
                spot = pl.ds(t * LANES, LANES)
                miss = [proj[i, rows, cols] for i in range(2)]
                for f in range(3):
                    z = zslot[f, rows, spot]
                    for i in range(2):
                        miss[i] = miss[i] - jp[3 * i + f, rows, cols].astype(F32) * z
                push = [
                    jc[k, rows, cols].astype(F32) * miss[0]
                    + jc[9 + k, rows, cols].astype(F32) * miss[1]
                    for k in range(9)
                ]
                upper = jnp.where(idx[rows, cols] >= BLOCK // 2, 1.0, 0.0)
                for h in range(2):
                    mine = [value[h * 8 : h * 8 + 8] for value in push]
                    last_high = mine[8].astype(BF16).astype(F32)
                    halves = upper[h * 8 : h * 8 + 8]
                    halves = jnp.concatenate([halves, halves], axis=0).astype(BF16) > 0.5
                    tiles = [None] * 9
                    for i in range(4):
                        pair = jnp.concatenate([mine[2 * i], mine[2 * i + 1]], axis=0)
                        tiles[i], tiles[5 + i] = split2(pair)
                    pair = jnp.concatenate([last_high, mine[8] - last_high], axis=0)
                    tiles[4] = pair.astype(BF16)
                    for i, value in enumerate(tiles):
                        pbuf[h, 16 * i : 16 * i + 16, spot] = value
                        above = jnp.where(halves, value, jnp.zeros_like(value))
                        pbuf[h, 144 + 16 * i : 160 + 16 * i, spot] = above

        def scatter(g):
            base = g * 16
            for h in range(2):
                total = None
                for t in range(width // KCOLS):
                    cols = pl.ds(c * width + t * KCOLS, KCOLS)
                    hot_rows = pl.ds(pl.multiple_of((base + h * 8) * (BLOCK // 2), 256), 4 * BLOCK)
                    piece = lax.dot_general(
                        pbuf[h, :, t * KCOLS : (t + 1) * KCOLS],
                        hots[hot_rows, cols],
                        (((1,), (1,)), ((), ())),
                        preferred_element_type=F32,
                    )
                    total = piece if total is None else total + piece
                if c == 0:
                    acc[2 * g + h] = total
                else:
                    acc[2 * g + h] += total

        groups = pairs // 16

        def group(g, carry):
            build(g)
            scatter(g)
            return carry

        lax.fori_loop(0, groups, group, 0)

    def slot_sums(first, last):
        small = (8, LANES)
        row = iota(small, 0)
        quarter = iota(small, 1) // (BLOCK // 2)
        first4 = row < 4
        turn = lax.rem(row, 4)

        def one(g, carry):
            rows = pl.ds(pl.multiple_of(g * 8, 8), 8)
            for i in range(first, last):
                line = jnp.zeros(small, F32)
                for q in range(4 if i < 4 else 2):
                    f = 2 * i + q // 2
                    if q % 2 == 0:
                        parts = []
                        for top in (0, 144):
                            low = top + (72 if f == 8 else 80 + 8 * f)
                            parts.append(
                                acc[g, top + 8 * f : top + 8 * f + 8, :] + acc[g, low : low + 8, :]
                            )
                    both = parts[0] - parts[1] if q % 2 == 0 else parts[1]
                    here = jnp.where(first4, both[:, :LANES], both[:, LANES:])
                    moved = None
                    for k in range(4):
                        shift = (32 * (q - k)) % LANES
                        turned = pltpu.roll(here, shift, 1) if shift else here
                        moved = turned if k == 0 else jnp.where(turn == k, turned, moved)
                    line = jnp.where(quarter == q, moved, line)
                slotsum[rows, i * LANES : (i + 1) * LANES] = line
            return carry

        lax.fori_loop(0, pairs // 8, one, 0)

    def schur(vec, it, a_copies, beside):
        wait_all(a_copies)
        make_tables(it)
        next(beside, None)
        first, second, third, fourth = {}, {}, {}, {}
        for step in range(CHUNKS + 4):
            if step < CHUNKS:
                first[step] = forward(step, it)
                next(beside, None)
            if 0 <= step - 1 < CHUNKS:
                second[step - 1] = reduce_sibling(step - 1, it, first[step - 1])
            if 0 <= step - 2 < CHUNKS:
                third[step - 2] = eliminate(step - 2, it, second[step - 2])
            if 0 <= step - 3 < CHUNKS:
                fourth[step - 3] = share(step - 3, it, third[step - 3])
            if step - 4 >= 0:
                backward(step - 4, it, fourth[step - 4])
        copies = []
        for n, (first, last) in enumerate(((0, 2), (2, 5))):
            slot_sums(first, last)
            high, low = split2(slotsum[:, first * LANES : last * LANES])
            rows = slice(first * cap, last * cap if n == 0 else 4 * cap + cap // 2)
            pack(
                dot(pick[...], jnp.concatenate([high, low], axis=0)), out_pack.at[it], first, last
            )
            copies += pt_exchange(
                lambda peer: out_pack.at[it, peer, rows], in_pack.at[it, me_pt, rows],
                e_send.at[it, n], e_recv.at[it, n],
            )
        in_pack[it, me_pt] = out_pack[it, me_pt]
        next(beside, None)
        wait_all(copies)
        high, low = split2(unpack(in_pack.at[it]))
        total = dot(place_t[...], high) + dot(place_t[...], low)
        return damp[...] * vec[...] + total

    def fill(value):
        return jnp.broadcast_to(jnp.sum(value, keepdims=True), (8, LANES))

    def start_dots(values, n):
        for k, value in enumerate(values):
            dots[n, k] = fill(value)
        copies = []
        for hop in range(1, owners):
            copy = pltpu.make_async_remote_copy(
                src_ref=dots.at[n], dst_ref=dots_pt.at[n, hop - 1],
                send_sem=dp_sem.at[0, n, hop - 1], recv_sem=dp_sem.at[1, n, hop - 1],
                device_id=at_pt(lax.rem(me_pt + hop, owners)), device_id_type=MESH,
            )
            copy.start()
            copies.append(copy)
        return copies

    def pass_dots(copies, n):
        wait_all(copies)
        total = dots[n]
        for hop in range(1, owners):
            total = total + dots_pt[n, hop - 1]
        dots_cam[n, 0] = total
        copies = []
        for hop in range(1, ncam):
            copy = pltpu.make_async_remote_copy(
                src_ref=dots_cam.at[n, 0], dst_ref=dots_cam.at[n, hop],
                send_sem=dc_sem.at[0, n, hop - 1], recv_sem=dc_sem.at[1, n, hop - 1],
                device_id=at_cam(lax.rem(me_cam + hop, ncam)), device_id_type=MESH,
            )
            copy.start()
            copies.append(copy)
        return copies

    def end_dots(copies, n, k):
        wait_all(copies)
        total = dots_cam[n, 0]
        for hop in range(1, ncam):
            total = total + dots_cam[n, hop]
        return [total[i][0:1, 0:1] for i in range(k)]

    v1[...] = schur(v0, 0, a_copies, iter(()))
    a_copies = send_blocks(v1, 1)
    known = []

    def scalars(copies):
        copies = pass_dots(copies, 0)
        yield
        yield
        norm0, curve0 = end_dots(copies, 0, 2)
        step0 = norm0 / curve0
        res1 = v0[...] - step0 * v1[...]
        copies = start_dots([res1 * res1], 1)
        yield
        yield
        copies = pass_dots(copies, 1)
        yield
        (norm1,) = end_dots(copies, 1, 1)
        known.extend([norm0, norm1, step0])
        yield

    copies = start_dots([v0[...] * v0[...], v0[...] * v1[...]], 0)
    v2[...] = schur(v1, 1, a_copies, scalars(copies))
    norm0, norm1, step0 = known
    res1 = v0[...] - step0 * v1[...]
    ratio = norm1 / norm0
    dir1 = res1 + ratio * v0[...]
    image1 = v1[...] - step0 * v2[...] + ratio * v1[...]
    three = start_dots([dir1 * image1], 2)
    three = pass_dots(three, 2)
    (curve1,) = end_dots(three, 2, 1)
    step1 = norm1 / curve1
    from_rows(step0 * v0[...] + step1 * dir1, answer_ref)
    from_rows(res1 - step1 * image1, residual_ref)


def per_device(
    right_side, cam_damping, point_damping, block_ids, slab_ids, cam_index, cam_jacobian,
    point_jacobian, pair_count,
):
    pairs = block_ids.shape[2]
    points = cam_index.shape[3]
    slabs = point_damping.shape[0] // points
    cam_dev = right_side.shape[1]
    blocks_dev = cam_dev // BLOCK
    owners = lax.axis_size("pt")
    ncam = lax.axis_size("cam")
    nx = ncam // 2
    spots = 2 * pairs
    cap = spots // owners
    width = points // CHUNKS
    part = width // ncam
    idx = cam_index.reshape(pairs, points)
    jc = cam_jacobian.reshape(pairs, 18, points).transpose(1, 0, 2)
    jp = point_jacobian.reshape(pairs, 6, points).transpose(1, 0, 2)
    vmem = pl.BlockSpec(memory_space=pltpu.VMEM)
    hbm = pl.BlockSpec(memory_space=pl.ANY)
    V = pltpu.VMEM
    D = pltpu.SemaphoreType.DMA
    far = max(nx - 1, 1)
    scratch = [
        V((pairs, points), jnp.int32), V((18, pairs, points), BF16), V((6, pairs, points), BF16),
        V((pairs * BLOCK // 2, points), BF16),
        D((2 * CHUNKS + 1,)),
        V((spots, blocks_dev), BF16), V((blocks_dev, spots), BF16),
        V((spots, 2 * pairs), BF16), V((pairs, spots), BF16),
        V((slabs, 2 * pairs), BF16), V((pairs, 2 * slabs), BF16),
        V((owners, cap, LANES), F32), V((owners, cap, LANES), F32),
        V((9 * blocks_dev // 2, LANES), F32),
        V((blocks_dev, COLS), F32), V((blocks_dev, COLS), F32), V((blocks_dev, COLS), F32),
        V((blocks_dev, COLS), F32),
        V((ITERS, owners, 4 * cap + cap // 2, LANES), F32),
        V((ITERS, owners, 4 * cap + cap // 2, LANES), F32),
        V((9, pairs, LANES), F32),
        V((2, pairs, points), F32),
        V((6, 2 * pairs, width), BF16),
        V((3, pairs, width), F32),
        V((2, 288, width), BF16),
        V((pairs // 8, 288, 4 * BLOCK), F32),
        V((pairs, COLS), F32),
        V((CHUNKS, 2, nx, 6, slabs, part), F32), V((CHUNKS, nx, 6, slabs, part), F32),
        V((CHUNKS, nx, 6, slabs, part), F32), V((CHUNKS, far, 6, slabs, part), F32),
        V((CHUNKS, 6, slabs, part), F32),
        V((ITERS, CHUNKS, 2, nx, 3, slabs, part), F32), V((ITERS, CHUNKS, nx, 3, slabs, part), F32),
        V((ITERS, CHUNKS, nx, 3, slabs, part), F32), V((ITERS, CHUNKS, far, 3, slabs, part), F32),
        V((ITERS, CHUNKS, 2, nx, 3, slabs, part), F32),
        V((ITERS, owners, 4 * cap + cap // 2, LANES), F32),
        V((ITERS, owners, 4 * cap + cap // 2, LANES), F32),
        V((3, 2, 8, LANES), F32), V((3, owners - 1, 2, 8, LANES), F32),
        V((3, ncam, 2, 8, LANES), F32),
        D((owners - 1,)), D((owners - 1,)),
        D((ITERS, owners - 1)), D((ITERS, owners - 1)),
        D((ITERS, 2, owners - 1)), D((ITERS, 2, owners - 1)),
        D((2, CHUNKS)), D((2, CHUNKS, far)),
        D((ITERS, 2, CHUNKS)), D((ITERS, 2, CHUNKS, far)),
        D((ITERS, 2, CHUNKS, far)), D((ITERS, 2, CHUNKS)),
        D((2, 3, owners - 1)), D((2, 3, ncam - 1)),
    ]
    outs = pl.pallas_call(
        body,
        name="cg",
        out_shape=[jax.ShapeDtypeStruct((9, blocks_dev // 2, LANES), F32)] * 2,
        in_specs=[vmem] * 6 + [hbm] * 3,
        out_specs=[vmem] * 2,
        scratch_shapes=scratch,
        compiler_params=pltpu.CompilerParams(
            collective_id=0, has_side_effects=True, vmem_limit_bytes=VMEM_BYTES
        ),
    )(
        block_ids.reshape(1, pairs), slab_ids.reshape(1, pairs), pair_count.reshape(1, 1),
        right_side, cam_damping, point_damping.reshape(-1, LANES), idx, jc, jp,
    )
    return outs[0].reshape(9, cam_dev), outs[1].reshape(9, cam_dev)


def solution(mesh):
    in_specs = (
        P(None, ("cam", "pt")),
        P(None, ("cam", "pt")),
        P("pt"),
        P("cam", "pt", None),
        P("cam", "pt", None),
        P("cam", "pt", None, None),
        P("cam", "pt", None, None, None),
        P("cam", "pt", None, None, None),
        P("cam", "pt"),
    )
    out_specs = (P(None, ("cam", "pt")), P(None, ("cam", "pt")))
    return jax.shard_map(
        per_device, mesh=mesh, in_specs=in_specs, out_specs=out_specs, check_vma=False
    )
```
